32 devices in a mesh: req: 8 (over z, y), tp: 4 (over x, core).
Axes of the slice: x: 2, y: 2, z: 4, core: 2. Of those that a mesh axis runs over, the one named last changes fastest.
Arguments:
- tokens: bfloat16 [4096, 2048], P('req')
- token_request_number: int32 [8, 512], P('req'), may hold values from 0 to 7, never falling along the last dimension, each value on 1 to 256 neighbouring positions
- request_adapter_position: int32 [8, 8], P('req'), may hold values from 0 to 15
- adapters_in_use: int32 [16], replicated, may hold values from 0 to 15, as said below
- adapter_storage_slot: int32 [16], replicated, may hold values from 0 to 15, each once
- input_norm_gain: bfloat16 [2048], replicated, may hold values from 0.5 to 1.5
- query_weight: bfloat16 [2048, 2048], P('req', 'tp')
- key_weight: bfloat16 [2048, 2048], P('req', 'tp')
- value_weight: bfloat16 [2048, 2048], P('req', 'tp'), may hold values from -0.125 to 0.125
- output_weight: bfloat16 [2048, 2048], P('tp', 'req'), may hold values from -0.125 to 0.125
- adapter_down_weight: bfloat16 [16, 2, 16, 2048], P('req'), may hold values from -0.125 to 0.125
- adapter_up_weight: bfloat16 [16, 2, 16, 2048], P('req', None, None, 'tp'), may hold values from -0.75 to 0.75
Outputs:
- layer_out: bfloat16 [4096, 2048], P('req', 'tp')
The draws below stay inside these ranges and needn't reach their ends.
Inputs may be any that keep to these rules, and one draw needn't show every extreme that they name: `adapters_in_use`: 16 different adapter numbers; 0 and 15 are always among them. `token_request_number`: the 512 tokens of each index of req form exactly 8 requests in order, each of 1 to 256 tokens, and one of exactly 256.
All inputs are finite; a program needn't handle non-finite values.
Results may differ from the reference program's by a relative error of at most 0.01.
Values may be sent and summed in bfloat16 or wider, within the bound.
A program may use at most 64 MiB of HBM per device.

```python
import math
import jax
import jax.numpy as jnp
import numpy as np
from jax import lax

MODEL_WIDTH = 2048
ATTENTION_HEADS = 32
HEAD_WIDTH = 64
ADAPTER_RANK = 16
ACTIVE = 16
PROMPT_TOKENS = 512
REQ_DEV = 8
MOST_LEN = 256
TOKENS = 4096
STORED_ADAPTERS = 16
N_REQ = 8


def shared_query(key):
    return jax.random.normal(jax.random.fold_in(key, 11), (MODEL_WIDTH, MODEL_WIDTH), jnp.float32) * MODEL_WIDTH ** (-0.5)


def draw_query_weight(key, part):
    return shared_query(key).astype(jnp.bfloat16)


def draw_key_weight(key, part):
    own_part = jax.random.normal(jax.random.fold_in(key, 12), (MODEL_WIDTH, MODEL_WIDTH), jnp.float32) * MODEL_WIDTH ** (-0.5)
    return own_part.astype(jnp.bfloat16)


def draw_tokens(key, part):
    base = jax.random.normal(jax.random.fold_in(key, 21), (TOKENS, MODEL_WIDTH), jnp.float32)
    return jnp.clip(base, -6.0, 6.0).astype(jnp.bfloat16)


def draw_adapters_in_use(key, part):
    middle = jax.random.permutation(jax.random.fold_in(key, 31), STORED_ADAPTERS - 2).astype(jnp.int32) + 1
    chosen = jnp.concatenate([jnp.array([0, STORED_ADAPTERS - 1], jnp.int32), middle[:ACTIVE - 2]])
    return jax.random.permutation(jax.random.fold_in(key, 32), chosen).astype(jnp.int32)


def set_ends(drawn, stream_key, least, largest):
    longest = drawn.shape.index(max(drawn.shape))
    spots = []
    for shift in (0, 1):
        where = [jax.random.randint(jax.random.fold_in(stream_key, axis), (), 0, length) for axis, length in enumerate(drawn.shape)]
        where[longest] = (where[longest] + shift) % drawn.shape[longest]
        spots.append(tuple(where))
    return drawn.at[spots[0]].set(least).at[spots[1]].set(largest)


def levels(stream_key, shape, shards, least, top_value):
    level, own = 1.0, jax.random.fold_in(stream_key, 6)
    for dim, shards_of in shards:
        heights = jnp.exp(jax.random.uniform(jax.random.fold_in(own, dim), (shards_of,), jnp.float32, least / len(shards), top_value / len(shards)))
        level = level * jnp.repeat(heights, shape[dim] // shards_of).reshape([-1 if axis == dim else 1 for axis in range(len(shape))])
    return level


def split_up(amount, total, limit, skew):
    portions = [(1 << 20) // math.isqrt(grade ** skew) + 1 for grade in range(2, amount + 1)]
    spare, holding = total - limit - (amount - 1), [1] * (amount - 1)
    while spare > 0:
        candidates = [i for i in range(amount - 1) if holding[i] < limit]
        pool, left = sum([portions[i] for i in candidates]), spare
        for i in candidates:
            more = min(limit - holding[i], max(1, left * portions[i] // pool), spare)
            holding[i] = holding[i] + more
            spare = spare - more
    return np.array([limit] + holding)


def uneven(own_key, number_of, total, most, lean):
    if number_of == 2:
        one = jax.random.randint(own_key, (), max(1, total - most), min(most, total - 1) + 1)
        return jnp.stack([one, total - one])
    lengths = jnp.asarray(split_up(number_of, total, most, lean), jnp.int32)
    twos = (number_of - 1) // 2
    giver, taker = lengths[1:1 + 2 * twos:2], lengths[2:2 + 2 * twos:2]
    slack = jnp.minimum(giver - 1, most - taker)
    shifted = jax.random.randint(jax.random.fold_in(own_key, 1), (twos,), 0, 1 << 20) % (slack + 1)
    lengths = lengths.at[1:1 + 2 * twos:2].set(giver - shifted).at[2:2 + 2 * twos:2].set(taker + shifted)
    return lengths[jax.random.permutation(jax.random.fold_in(own_key, 2), number_of)]


def bell_draw(rng, dims, scale, reach, pieces=(), kind=jnp.bfloat16):
    factor_of = levels(rng, dims, pieces, -0.22, 0.18) if pieces else 1.0
    drawn = jax.random.normal(rng, dims, jnp.float32) * scale * factor_of
    return jnp.minimum(jnp.maximum(drawn, -reach), reach).astype(kind)


def setup_inputs(seed: int = 0) -> dict:
    key_list = jax.random.split(jax.random.key(seed), 13)
    return {
        "tokens": draw_tokens(jax.random.fold_in(key_list[12], 71), 0),
        "token_request_number": jax.vmap(lambda own: jnp.searchsorted(jnp.cumsum(uneven(own, REQ_DEV, PROMPT_TOKENS, MOST_LEN, 2)), jnp.arange(PROMPT_TOKENS), side="right"))(jax.random.split(key_list[1], N_REQ)).reshape((N_REQ, PROMPT_TOKENS)).astype(jnp.int32),
        "request_adapter_position": set_ends(jax.random.randint(key_list[2], (N_REQ, REQ_DEV), 0, ACTIVE), jax.random.fold_in(key_list[2], 1), 0, ACTIVE - 1).astype(jnp.int32),
        "adapters_in_use": draw_adapters_in_use(jax.random.fold_in(key_list[12], 71), 0),
        "adapter_storage_slot": jax.random.permutation(key_list[4], STORED_ADAPTERS).astype(jnp.int32),
        "input_norm_gain": jnp.clip(jax.random.uniform(key_list[5], (MODEL_WIDTH,), jnp.float32, 0.5, 1.5), 0.5, 1.5).astype(jnp.bfloat16),
        "query_weight": draw_query_weight(jax.random.fold_in(key_list[12], 71), 0),
        "key_weight": draw_key_weight(jax.random.fold_in(key_list[12], 71), 0),
        "value_weight": bell_draw(key_list[8], (MODEL_WIDTH, MODEL_WIDTH), MODEL_WIDTH ** -0.5, 0.125, ((0, 8), (1, 4))),
        "output_weight": bell_draw(key_list[9], (MODEL_WIDTH, MODEL_WIDTH), MODEL_WIDTH ** -0.5, 0.125, ((0, 4), (1, 8))),
        "adapter_down_weight": bell_draw(key_list[10], (STORED_ADAPTERS, 2, ADAPTER_RANK, MODEL_WIDTH), MODEL_WIDTH ** -0.5, 0.125, ((0, 8),)),
        "adapter_up_weight": bell_draw(key_list[11], (STORED_ADAPTERS, 2, ADAPTER_RANK, MODEL_WIDTH), (4 * ADAPTER_RANK) ** -0.5, 0.75, ((0, 8), (3, 4))),
    }


norm_eps = 1e-05
rope_base = 130000.0
adapter_scale = 2.0

def positions_of(segment):
    ordinal = jnp.arange(segment.shape[0], dtype=jnp.int32)
    starts = jnp.concatenate([jnp.ones((1,), jnp.bool_), segment[1:] != segment[:-1]])
    segment_start = lax.cummax(jnp.where(starts, ordinal, jnp.zeros_like(ordinal)), axis=0)
    return ordinal - segment_start

def apply_rotation(values, token_positions):
    half_dim = HEAD_WIDTH // 2
    frequency = rope_base ** (-(jnp.arange(half_dim, dtype=jnp.float32) * 2.0 / HEAD_WIDTH))
    angles = token_positions.astype(jnp.float32)[:, None] * frequency[None, :]
    cosine = jnp.cos(angles)[:, None, :]
    sine_part = jnp.sin(angles)[:, None, :]
    first_half = values[..., :half_dim]
    second_half = values[..., half_dim:]
    return jnp.concatenate([first_half * cosine - second_half * sine_part, second_half * cosine + first_half * sine_part], axis=-1)

def attend(query_per_head, key_heads, value_per_head, segment):
    scores = jnp.einsum('qhd,khd->hqk', query_per_head.astype(jnp.float32), key_heads.astype(jnp.float32)) * 0.125
    ordinal = jnp.arange(segment.shape[0], dtype=jnp.int32)
    allowed = (segment[:, None] == segment[None, :]) & (ordinal[None, :] <= ordinal[:, None])
    scores = jnp.where(allowed[None], scores, jnp.float32(-1e+30))
    row_peak = lax.optimization_barrier(jnp.max(scores, axis=-1, keepdims=True))
    exponent = jnp.where(allowed[None], jnp.exp(scores - row_peak), jnp.float32(0.0))
    weights = (exponent / lax.optimization_barrier(jnp.sum(exponent, axis=-1, keepdims=True))).astype(jnp.bfloat16)
    return jnp.einsum('hqk,khd->qhd', weights.astype(jnp.float32), value_per_head.astype(jnp.float32)).astype(jnp.bfloat16)

def reference(tokens, token_request_number, request_adapter_position, adapters_in_use, adapter_storage_slot, input_norm_gain, query_weight, key_weight, value_weight, output_weight, adapter_down_weight, adapter_up_weight):
    storage_slots = jnp.take(adapter_storage_slot, adapters_in_use, axis=0).astype(jnp.int32)
    in_use_down = jnp.take(adapter_down_weight, storage_slots, axis=0)
    in_use_up = jnp.take(adapter_up_weight, storage_slots, axis=0)
    down_matrix = in_use_down.reshape(ACTIVE * 2 * ADAPTER_RANK, MODEL_WIDTH)
    blocks = tokens.reshape(N_REQ, PROMPT_TOKENS, MODEL_WIDTH)

    def one_block(block):
        rows, segment, request_adapters = block
        floats = rows.astype(jnp.float32)
        normed = (floats * lax.rsqrt(lax.optimization_barrier(jnp.mean(floats * floats, axis=-1, keepdims=True)) + norm_eps) * input_norm_gain.astype(jnp.float32)).astype(jnp.bfloat16)
        query_plain = jnp.dot(normed, query_weight, preferred_element_type=jnp.float32)
        key_base = jnp.dot(normed, key_weight, preferred_element_type=jnp.float32)
        value_plain = jnp.dot(normed, value_weight, preferred_element_type=jnp.float32)
        member = segment[:, None] == jnp.arange(REQ_DEV, dtype=jnp.int32)[None, :]
        token_adapter = lax.optimization_barrier(jnp.sum(jnp.where(member, request_adapters[None, :], jnp.zeros_like(request_adapters)[None, :]), axis=1))
        select = token_adapter[:, None] == jnp.arange(ACTIVE, dtype=jnp.int32)[None, :]
        shrunk_all = lax.dot_general(normed, down_matrix, (((1,), (1,)), ((), ())), preferred_element_type=jnp.float32).reshape(PROMPT_TOKENS, ACTIVE, 2, ADAPTER_RANK)
        shrunk = lax.optimization_barrier(jnp.sum(jnp.where(select[:, :, None, None], shrunk_all, jnp.float32(0.0)), axis=1)).astype(jnp.bfloat16)
        spread = jnp.where(select[:, :, None, None], shrunk[:, None, :, :], jnp.zeros((), jnp.bfloat16))
        query_change = jnp.dot(spread[:, :, 0, :].reshape(PROMPT_TOKENS, ACTIVE * ADAPTER_RANK), in_use_up[:, 0].reshape(ACTIVE * ADAPTER_RANK, MODEL_WIDTH), preferred_element_type=jnp.float32)
        value_change = jnp.dot(spread[:, :, 1, :].reshape(PROMPT_TOKENS, ACTIVE * ADAPTER_RANK), in_use_up[:, 1].reshape(ACTIVE * ADAPTER_RANK, MODEL_WIDTH), preferred_element_type=jnp.float32)
        token_positions = positions_of(segment)
        query_per_head = apply_rotation((query_plain + adapter_scale * query_change).reshape(PROMPT_TOKENS, ATTENTION_HEADS, HEAD_WIDTH), token_positions).astype(jnp.bfloat16)
        key_heads = apply_rotation(key_base.reshape(PROMPT_TOKENS, ATTENTION_HEADS, HEAD_WIDTH), token_positions).astype(jnp.bfloat16)
        value_per_head = (value_plain + adapter_scale * value_change).astype(jnp.bfloat16).reshape(PROMPT_TOKENS, ATTENTION_HEADS, HEAD_WIDTH)
        attended = attend(query_per_head, key_heads, value_per_head, segment).reshape(PROMPT_TOKENS, MODEL_WIDTH)
        return (floats + jnp.dot(attended, output_weight, preferred_element_type=jnp.float32)).astype(jnp.bfloat16)
    outputs = lax.map(one_block, (blocks, token_request_number, request_adapter_position))
    return outputs.reshape(N_REQ * PROMPT_TOKENS, MODEL_WIDTH)
```

```python
import jax
import jax.numpy as jnp
from jax import lax
from jax.sharding import PartitionSpec as P

HEAD_WIDTH = 64


norm_eps = 1e-05
rope_base = 130000.0
adapter_scale = 2.0


def fetch_adapters(down_part, up_part, active_slots, request_adapters, req_total):
    slot_total = down_part.shape[0]
    stored = jnp.concatenate([down_part, up_part], axis=1)
    split = down_part.shape[1]
    if slot_total * req_total <= 2 * active_slots.shape[0]:
        fetched = lax.all_gather(stored, "req", axis=0, tiled=True)
        places = active_slots[request_adapters]
    else:
        own = (active_slots // slot_total) == lax.axis_index("req")
        rows = jnp.where(
            own[:, None],
            jnp.take(stored, active_slots % slot_total, axis=0),
            jnp.zeros((), stored.dtype),
        )
        fetched = lax.psum(rows, "req")
        places = request_adapters
    return fetched[:, :split], fetched[:, split:], places


def positions_of(segment):
    ordinal = jnp.arange(segment.shape[0], dtype=jnp.int32)
    starts = jnp.concatenate([jnp.ones((1,), jnp.bool_), segment[1:] != segment[:-1]])
    segment_start = lax.cummax(jnp.where(starts, ordinal, jnp.zeros_like(ordinal)), axis=0)
    return ordinal - segment_start


def apply_rotation(values, token_positions):
    half_dim = HEAD_WIDTH // 2
    frequency = rope_base ** (-(jnp.arange(half_dim, dtype=jnp.float32) * 2.0 / HEAD_WIDTH))
    angles = token_positions.astype(jnp.float32)[:, None] * frequency[None, :]
    cosine = jnp.cos(angles)[:, None, :]
    sine_part = jnp.sin(angles)[:, None, :]
    first_half = values[..., :half_dim]
    second_half = values[..., half_dim:]
    return jnp.concatenate(
        [
            first_half * cosine - second_half * sine_part,
            second_half * cosine + first_half * sine_part,
        ],
        axis=-1,
    )


def attend(query_per_head, key_heads, value_per_head, segment):
    scores = (
        jnp.einsum("qhd,khd->hqk", query_per_head, key_heads, preferred_element_type=jnp.float32)
        * 0.125
    )
    ordinal = jnp.arange(segment.shape[0], dtype=jnp.int32)
    allowed = (segment[:, None] == segment[None, :]) & (ordinal[None, :] <= ordinal[:, None])
    scores = jnp.where(allowed[None], scores, jnp.float32(-1e30))
    row_peak = jnp.max(scores, axis=-1, keepdims=True)
    exponent = jnp.where(allowed[None], jnp.exp(scores - row_peak), jnp.float32(0.0))
    weights = (exponent / jnp.sum(exponent, axis=-1, keepdims=True)).astype(jnp.bfloat16)
    return jnp.einsum(
        "hqk,khd->qhd", weights, value_per_head, preferred_element_type=jnp.float32
    ).astype(jnp.bfloat16)


def local(
    tokens,
    token_request_number,
    request_adapter_position,
    adapters_in_use,
    adapter_storage_slot,
    input_norm_gain,
    query_weight,
    key_weight,
    value_weight,
    output_weight,
    adapter_down_weight,
    adapter_up_weight,
):
    row_total, model_width = tokens.shape
    local_width = query_weight.shape[1]
    reduced_rows = adapter_down_weight.shape[2]
    active_count = adapters_in_use.shape[0]
    slot_total = adapter_down_weight.shape[0]
    segment = token_request_number[0]
    request_adapters = request_adapter_position[0]
    tp_total = lax.axis_size("tp")
    req_total = lax.axis_size("req")
    part_rows = reduced_rows // tp_total
    down_part = lax.dynamic_slice_in_dim(
        adapter_down_weight, lax.axis_index("tp") * part_rows, part_rows, 2
    ).reshape(slot_total, 2 * part_rows * model_width)
    up_part = adapter_up_weight.reshape(slot_total, 2 * reduced_rows * local_width)
    down_all, up_all, request_places = fetch_adapters(
        down_part,
        up_part,
        jnp.take(adapter_storage_slot, adapters_in_use, axis=0),
        request_adapters,
        req_total,
    )
    place_total = down_all.shape[0]
    floats = tokens.astype(jnp.float32)
    normed = (
        floats
        * lax.rsqrt(jnp.mean(floats * floats, axis=-1, keepdims=True) + norm_eps)
        * input_norm_gain.astype(jnp.float32)
    ).astype(jnp.bfloat16)
    query_plain = jnp.dot(
        normed,
        lax.all_gather(query_weight, "req", axis=0, tiled=True),
        preferred_element_type=jnp.float32,
    )
    key_base = jnp.dot(
        normed,
        lax.all_gather(key_weight, "req", axis=0, tiled=True),
        preferred_element_type=jnp.float32,
    )
    value_plain = jnp.dot(
        normed,
        lax.all_gather(value_weight, "req", axis=0, tiled=True),
        preferred_element_type=jnp.float32,
    )
    request_total = request_adapters.shape[0]
    member = segment[:, None] == jnp.arange(request_total, dtype=jnp.int32)[None, :]
    token_place = jnp.sum(
        jnp.where(member, request_places[None, :], jnp.zeros_like(request_places)[None, :]),
        axis=1,
    )
    share = 2 * part_rows
    shrunk_all = lax.dot_general(
        normed,
        down_all.reshape(place_total * share, model_width),
        (((1,), (1,)), ((), ())),
        preferred_element_type=jnp.float32,
    ).astype(jnp.bfloat16)
    column = jnp.arange(place_total * share, dtype=jnp.int32)
    kept = jnp.where(
        token_place[:, None] == (column // share)[None, :], shrunk_all, jnp.zeros((), jnp.bfloat16)
    )
    fold = (column % share)[:, None] == jnp.arange(share, dtype=jnp.int32)[None, :]
    shrunk_part = jnp.dot(
        kept, fold.astype(jnp.bfloat16), preferred_element_type=jnp.float32
    ).astype(jnp.bfloat16)
    shrunk = lax.all_gather(shrunk_part, "tp", axis=1, tiled=True)
    source = jnp.arange(tp_total * share, dtype=jnp.int32)
    source_kind = (source % share) // part_rows
    source_rank = (source // share) * part_rows + source % part_rows
    target = jnp.arange(place_total * reduced_rows, dtype=jnp.int32)
    mine = token_place[:, None] == (target // reduced_rows)[None, :]
    up_all = up_all.reshape(place_total, 2, reduced_rows, local_width)

    def change_of(kind):
        spread_map = (source_kind == kind)[:, None] & (
            source_rank[:, None] == (target % reduced_rows)[None, :]
        )
        spread = jnp.dot(
            shrunk, spread_map.astype(jnp.bfloat16), preferred_element_type=jnp.float32
        ).astype(jnp.bfloat16)
        spread = jnp.where(mine, spread, jnp.zeros((), jnp.bfloat16))
        return jnp.dot(
            spread,
            up_all[:, kind].reshape(place_total * reduced_rows, local_width),
            preferred_element_type=jnp.float32,
        )

    query_change = change_of(0)
    value_change = change_of(1)
    head_total = local_width // HEAD_WIDTH
    token_positions = positions_of(segment)
    query_per_head = apply_rotation(
        (query_plain + adapter_scale * query_change).reshape(row_total, head_total, HEAD_WIDTH),
        token_positions,
    ).astype(jnp.bfloat16)
    key_heads = apply_rotation(
        key_base.reshape(row_total, head_total, HEAD_WIDTH), token_positions
    ).astype(jnp.bfloat16)
    value_per_head = (
        (value_plain + adapter_scale * value_change)
        .astype(jnp.bfloat16)
        .reshape(row_total, head_total, HEAD_WIDTH)
    )
    attended = attend(query_per_head, key_heads, value_per_head, segment).reshape(
        row_total, local_width
    )
    partial_out = jnp.dot(
        attended,
        lax.all_gather(output_weight, "req", axis=1, tiled=True),
        preferred_element_type=jnp.float32,
    )
    summed = lax.psum_scatter(
        partial_out.astype(jnp.bfloat16), "tp", scatter_dimension=1, tiled=True
    ).astype(jnp.float32)
    share_width = summed.shape[1]
    residual_part = lax.dynamic_slice_in_dim(
        tokens, lax.axis_index("tp") * share_width, share_width, 1
    )
    return (summed + residual_part.astype(jnp.float32)).astype(jnp.bfloat16)


def solution(mesh):
    in_specs = (
        P("req", None),
        P("req", None),
        P("req", None),
        P(),
        P(),
        P(),
        P("req", "tp"),
        P("req", "tp"),
        P("req", "tp"),
        P("tp", "req"),
        P("req", None, None, None),
        P("req", None, None, "tp"),
    )
    out_specs = P("req", "tp")
    return jax.shard_map(local, mesh=mesh, in_specs=in_specs, out_specs=out_specs, check_vma=False)
```

```python
import functools

import jax
import jax.numpy as jnp
from jax import lax
from jax.experimental import pallas as pl
from jax.experimental.pallas import tpu as pltpu
from jax.sharding import PartitionSpec as P

HEAD_WIDTH = 64


norm_eps = 1e-05
rope_base = 130000.0
adapter_scale = 2.0


def relay_kernel(lines, axes, *refs):
    count = len(axes)
    sources, gathered = refs[:count], refs[count : 2 * count]
    send_sems, recv_sems, local_sems = refs[2 * count :]
    me = lax.axis_index("req")
    line = lax.div(me, 2)
    side = lax.rem(me, 2)
    partner = 2 * line + 1 - side
    has_up = line < lines - 1
    has_down = line > 0

    def block(index, origin):
        if axes[index] == 0:
            return gathered[index].at[origin]
        width = sources[index].shape[1]
        return gathered[index].at[:, pl.ds(pl.multiple_of(origin * width, width), width)]

    def to_device(index, origin, slot, target):
        source = sources[index] if slot < 3 else block(index, origin)
        return pltpu.make_async_remote_copy(
            src_ref=source,
            dst_ref=block(index, origin),
            send_sem=send_sems.at[index, slot],
            recv_sem=recv_sems.at[index, origin],
            device_id={"req": target},
            device_id_type=pl.DeviceIdType.MESH,
        )

    def arrival(index, origin):
        to_device(index, origin, 3, partner).wait_recv()

    barrier = pltpu.get_barrier_semaphore()

    def greet(target):
        pl.semaphore_signal(
            barrier, inc=1, device_id={"req": target}, device_id_type=pl.DeviceIdType.MESH
        )

    greet(partner)
    pl.when(has_up)(lambda: greet(me + 2))
    pl.when(has_down)(lambda: greet(me - 2))
    pl.semaphore_wait(barrier, 1 + has_up.astype(jnp.int32) + has_down.astype(jnp.int32))

    for index in range(count):
        pl.when(has_up)(lambda: to_device(index, me, 0, me + 2).start())
        pl.when(has_down)(lambda: to_device(index, me, 1, me - 2).start())
        to_device(index, me, 2, partner).start()
    for index in range(count):
        pltpu.make_async_copy(sources[index], block(index, me), local_sems.at[index]).start()
    for step in range(1, lines):
        slot = 3 + 4 * (step - 1)
        for index in range(count):

            @pl.when(line >= step)
            def _():
                origin = me - 2 * step
                arrival(index, origin)
                pl.when(has_up)(lambda: to_device(index, origin, slot, me + 2).start())
                to_device(index, origin, slot + 1, partner).start()

            @pl.when(line + step < lines)
            def _():
                origin = me + 2 * step
                arrival(index, origin)
                pl.when(has_down)(lambda: to_device(index, origin, slot + 2, me - 2).start())
                to_device(index, origin, slot + 3, partner).start()

    for index in range(count):
        for other in range(lines):
            arrival(index, 2 * other + 1 - side)
        pltpu.make_async_copy(sources[index], block(index, me), local_sems.at[index]).wait()
        pl.when(has_up)(lambda: to_device(index, me, 0, me + 2).wait_send())
        pl.when(has_down)(lambda: to_device(index, me, 1, me - 2).wait_send())
        to_device(index, me, 2, partner).wait_send()
        for step in range(1, lines):
            slot = 3 + 4 * (step - 1)

            @pl.when(line >= step)
            def _():
                origin = me - 2 * step
                pl.when(has_up)(lambda: to_device(index, origin, slot, me + 2).wait_send())
                to_device(index, origin, slot + 1, partner).wait_send()

            @pl.when(line + step < lines)
            def _():
                origin = me + 2 * step
                pl.when(has_down)(lambda: to_device(index, origin, slot + 2, me - 2).wait_send())
                to_device(index, origin, slot + 3, partner).wait_send()


def relay_gather(arrays, axes, req_total):
    lines = req_total // 2
    count = len(arrays)
    shapes = []
    for array, axis in zip(arrays, axes):
        if axis == 0:
            shape = (req_total,) + array.shape
        else:
            shape = (array.shape[0], req_total * array.shape[1])
        shapes.append(jax.ShapeDtypeStruct(shape, array.dtype))
    return pl.pallas_call(
        functools.partial(relay_kernel, lines, tuple(axes)),
        out_shape=shapes,
        in_specs=[pl.BlockSpec(memory_space=pl.ANY)] * count,
        out_specs=[pl.BlockSpec(memory_space=pl.ANY)] * count,
        scratch_shapes=[
            pltpu.SemaphoreType.DMA((count, 3 + 4 * (lines - 1))),
            pltpu.SemaphoreType.DMA((count, req_total)),
            pltpu.SemaphoreType.DMA((count,)),
        ],
        compiler_params=pltpu.CompilerParams(collective_id=0, has_side_effects=True),
    )(*arrays)


def gather_all(arrays, axes, req_total):
    if req_total % 2 == 0 and req_total <= 16:
        gathered = relay_gather(arrays, axes, req_total)
    else:
        gathered = [
            lax.all_gather(array, "req", axis=axis, tiled=axis == 1)
            for array, axis in zip(arrays, axes)
        ]
    return [
        array.reshape((-1,) + array.shape[2:]) if axis == 0 else array
        for array, axis in zip(gathered, axes)
    ]


def active_rows(stored, active_slots):
    slot_total = stored.shape[0]
    own = (active_slots // slot_total) == lax.axis_index("req")
    rows = jnp.where(
        own[:, None, None],
        jnp.take(stored, active_slots % slot_total, axis=0),
        jnp.zeros((), stored.dtype),
    )
    return lax.psum(rows, "req").reshape(-1, stored.shape[2])


def positions_of(segment):
    ordinal = jnp.arange(segment.shape[0], dtype=jnp.int32)
    starts = jnp.concatenate([jnp.ones((1,), jnp.bool_), segment[1:] != segment[:-1]])
    segment_start = lax.cummax(jnp.where(starts, ordinal, jnp.zeros_like(ordinal)), axis=0)
    return ordinal - segment_start


def apply_rotation(values, token_positions):
    half_dim = HEAD_WIDTH // 2
    frequency = rope_base ** (-(jnp.arange(half_dim, dtype=jnp.float32) * 2.0 / HEAD_WIDTH))
    angles = token_positions.astype(jnp.float32)[:, None] * frequency[None, :]
    cosine = jnp.cos(angles)[:, None, :]
    sine_part = jnp.sin(angles)[:, None, :]
    first_half = values[..., :half_dim]
    second_half = values[..., half_dim:]
    return jnp.concatenate(
        [
            first_half * cosine - second_half * sine_part,
            second_half * cosine + first_half * sine_part,
        ],
        axis=-1,
    )


def attend(query_per_head, key_heads, value_per_head, segment):
    scores = (
        jnp.einsum("qhd,khd->hqk", query_per_head, key_heads, preferred_element_type=jnp.float32)
        * 0.125
    )
    ordinal = jnp.arange(segment.shape[0], dtype=jnp.int32)
    allowed = (segment[:, None] == segment[None, :]) & (ordinal[None, :] <= ordinal[:, None])
    scores = jnp.where(allowed[None], scores, jnp.float32(-1e30))
    row_peak = jnp.max(scores, axis=-1, keepdims=True)
    exponent = jnp.where(allowed[None], jnp.exp(scores - row_peak), jnp.float32(0.0))
    weights = (exponent / jnp.sum(exponent, axis=-1, keepdims=True)).astype(jnp.bfloat16)
    return jnp.einsum(
        "hqk,khd->qhd", weights, value_per_head, preferred_element_type=jnp.float32
    ).astype(jnp.bfloat16)


def local(
    tokens,
    token_request_number,
    request_adapter_position,
    adapters_in_use,
    adapter_storage_slot,
    input_norm_gain,
    query_weight,
    key_weight,
    value_weight,
    output_weight,
    adapter_down_weight,
    adapter_up_weight,
):
    row_total, model_width = tokens.shape
    local_width = query_weight.shape[1]
    reduced_rows = adapter_down_weight.shape[2]
    slot_total = adapter_down_weight.shape[0]
    segment = token_request_number[0]
    request_adapters = request_adapter_position[0]
    tp_total = lax.axis_size("tp")
    req_total = lax.axis_size("req")
    part_rows = reduced_rows // tp_total
    share = 2 * part_rows
    down_part = lax.dynamic_slice_in_dim(
        adapter_down_weight, lax.axis_index("tp") * part_rows, part_rows, 2
    ).reshape(slot_total, share, model_width)
    up_part = adapter_up_weight.reshape(slot_total, 2 * reduced_rows, local_width)
    active_slots = jnp.take(adapter_storage_slot, adapters_in_use, axis=0)
    arrays = [query_weight, key_weight, value_weight, output_weight]
    axes = [0, 0, 0, 1]
    if slot_total * req_total <= 2 * active_slots.shape[0]:
        adapter_parts = [
            down_part.reshape(slot_total * share, model_width),
            up_part.reshape(slot_total * 2 * reduced_rows, local_width),
        ]
        down_all, up_all, query_full, key_full, value_full, output_full = gather_all(
            adapter_parts + arrays, [0, 0] + axes, req_total
        )
        request_places = active_slots[request_adapters]
    else:
        down_all = active_rows(down_part, active_slots)
        up_all = active_rows(up_part, active_slots)
        query_full, key_full, value_full, output_full = gather_all(arrays, axes, req_total)
        request_places = request_adapters
    place_total = down_all.shape[0] // share
    floats = tokens.astype(jnp.float32)
    normed = (
        floats
        * lax.rsqrt(jnp.mean(floats * floats, axis=-1, keepdims=True) + norm_eps)
        * input_norm_gain.astype(jnp.float32)
    ).astype(jnp.bfloat16)
    query_plain = jnp.dot(
        normed,
        query_full,
        preferred_element_type=jnp.float32,
    )
    key_base = jnp.dot(
        normed,
        key_full,
        preferred_element_type=jnp.float32,
    )
    value_plain = jnp.dot(
        normed,
        value_full,
        preferred_element_type=jnp.float32,
    )
    request_total = request_adapters.shape[0]
    member = segment[:, None] == jnp.arange(request_total, dtype=jnp.int32)[None, :]
    token_place = jnp.sum(
        jnp.where(member, request_places[None, :], jnp.zeros_like(request_places)[None, :]),
        axis=1,
    )
    shrunk_all = lax.dot_general(
        normed,
        down_all,
        (((1,), (1,)), ((), ())),
        preferred_element_type=jnp.float32,
    ).astype(jnp.bfloat16)
    column = jnp.arange(place_total * share, dtype=jnp.int32)
    kept = jnp.where(
        token_place[:, None] == (column // share)[None, :], shrunk_all, jnp.zeros((), jnp.bfloat16)
    )
    fold = (column % share)[:, None] == jnp.arange(share, dtype=jnp.int32)[None, :]
    shrunk_part = jnp.dot(
        kept, fold.astype(jnp.bfloat16), preferred_element_type=jnp.float32
    ).astype(jnp.bfloat16)
    shrunk = lax.all_gather(shrunk_part, "tp", axis=1, tiled=True)
    source = jnp.arange(tp_total * share, dtype=jnp.int32)
    source_kind = (source % share) // part_rows
    source_rank = (source // share) * part_rows + source % part_rows
    target = jnp.arange(place_total * reduced_rows, dtype=jnp.int32)
    mine = token_place[:, None] == (target // reduced_rows)[None, :]
    up_all = up_all.reshape(place_total, 2, reduced_rows, local_width)

    def change_of(kind):
        spread_map = (source_kind == kind)[:, None] & (
            source_rank[:, None] == (target % reduced_rows)[None, :]
        )
        spread = jnp.dot(
            shrunk, spread_map.astype(jnp.bfloat16), preferred_element_type=jnp.float32
        ).astype(jnp.bfloat16)
        spread = jnp.where(mine, spread, jnp.zeros((), jnp.bfloat16))
        return jnp.dot(
            spread,
            up_all[:, kind].reshape(place_total * reduced_rows, local_width),
            preferred_element_type=jnp.float32,
        )

    query_change = change_of(0)
    value_change = change_of(1)
    head_total = local_width // HEAD_WIDTH
    token_positions = positions_of(segment)
    query_per_head = apply_rotation(
        (query_plain + adapter_scale * query_change).reshape(row_total, head_total, HEAD_WIDTH),
        token_positions,
    ).astype(jnp.bfloat16)
    key_heads = apply_rotation(
        key_base.reshape(row_total, head_total, HEAD_WIDTH), token_positions
    ).astype(jnp.bfloat16)
    value_per_head = (
        (value_plain + adapter_scale * value_change)
        .astype(jnp.bfloat16)
        .reshape(row_total, head_total, HEAD_WIDTH)
    )
    attended = attend(query_per_head, key_heads, value_per_head, segment).reshape(
        row_total, local_width
    )
    partial_out = jnp.dot(
        attended,
        output_full,
        preferred_element_type=jnp.float32,
    )
    summed = lax.psum_scatter(
        partial_out.astype(jnp.bfloat16), "tp", scatter_dimension=1, tiled=True
    ).astype(jnp.float32)
    share_width = summed.shape[1]
    residual_part = lax.dynamic_slice_in_dim(
        tokens, lax.axis_index("tp") * share_width, share_width, 1
    )
    return (summed + residual_part.astype(jnp.float32)).astype(jnp.bfloat16)


def solution(mesh):
    in_specs = (
        P("req", None),
        P("req", None),
        P("req", None),
        P(),
        P(),
        P(),
        P("req", "tp"),
        P("req", "tp"),
        P("req", "tp"),
        P("tp", "req"),
        P("req", None, None, None),
        P("req", None, None, "tp"),
    )
    out_specs = P("req", "tp")
    return jax.shard_map(local, mesh=mesh, in_specs=in_specs, out_specs=out_specs, check_vma=False)
```

```python
import functools

import jax
import jax.numpy as jnp
from jax import lax
from jax.experimental import pallas as pl
from jax.experimental.pallas import tpu as pltpu
from jax.sharding import PartitionSpec as P

HEAD_WIDTH = 64


norm_eps = 1e-05
rope_base = 130000.0
adapter_scale = 2.0


def relay_kernel(lines, axes, *refs):
    count = len(axes)
    sources, gathered = refs[:count], refs[count : 2 * count]
    send_sems, recv_sems, local_sems = refs[2 * count :]
    me = lax.axis_index("req")
    line = lax.div(me, 2)
    side = lax.rem(me, 2)
    partner = 2 * line + 1 - side
    has_up = line < lines - 1
    has_down = line > 0

    def block(index, origin):
        if axes[index] == 0:
            return gathered[index].at[origin]
        width = sources[index].shape[1]
        return gathered[index].at[:, pl.ds(pl.multiple_of(origin * width, width), width)]

    def to_device(index, origin, slot, target):
        source = sources[index] if slot < 3 else block(index, origin)
        return pltpu.make_async_remote_copy(
            src_ref=source,
            dst_ref=block(index, origin),
            send_sem=send_sems.at[index, slot],
            recv_sem=recv_sems.at[index, origin],
            device_id={"req": target},
            device_id_type=pl.DeviceIdType.MESH,
        )

    def arrival(index, origin):
        to_device(index, origin, 3, partner).wait_recv()

    barrier = pltpu.get_barrier_semaphore()

    def greet(target):
        pl.semaphore_signal(
            barrier, inc=1, device_id={"req": target}, device_id_type=pl.DeviceIdType.MESH
        )

    greet(partner)
    pl.when(has_up)(lambda: greet(me + 2))
    pl.when(has_down)(lambda: greet(me - 2))
    pl.semaphore_wait(barrier, 1 + has_up.astype(jnp.int32) + has_down.astype(jnp.int32))

    for index in range(count):
        pl.when(has_up)(lambda: to_device(index, me, 0, me + 2).start())
        pl.when(has_down)(lambda: to_device(index, me, 1, me - 2).start())
        to_device(index, me, 2, partner).start()
    for index in range(count):
        pltpu.make_async_copy(sources[index], block(index, me), local_sems.at[index]).start()
    for step in range(1, lines):
        slot = 3 + 4 * (step - 1)
        for index in range(count):

            @pl.when(line >= step)
            def _():
                origin = me - 2 * step
                arrival(index, origin)
                pl.when(has_up)(lambda: to_device(index, origin, slot, me + 2).start())
                to_device(index, origin, slot + 1, partner).start()

            @pl.when(line + step < lines)
            def _():
                origin = me + 2 * step
                arrival(index, origin)
                pl.when(has_down)(lambda: to_device(index, origin, slot + 2, me - 2).start())
                to_device(index, origin, slot + 3, partner).start()

    for index in range(count):
        for other in range(lines):
            arrival(index, 2 * other + 1 - side)
        pltpu.make_async_copy(sources[index], block(index, me), local_sems.at[index]).wait()
        pl.when(has_up)(lambda: to_device(index, me, 0, me + 2).wait_send())
        pl.when(has_down)(lambda: to_device(index, me, 1, me - 2).wait_send())
        to_device(index, me, 2, partner).wait_send()
        for step in range(1, lines):
            slot = 3 + 4 * (step - 1)

            @pl.when(line >= step)
            def _():
                origin = me - 2 * step
                pl.when(has_up)(lambda: to_device(index, origin, slot, me + 2).wait_send())
                to_device(index, origin, slot + 1, partner).wait_send()

            @pl.when(line + step < lines)
            def _():
                origin = me + 2 * step
                pl.when(has_down)(lambda: to_device(index, origin, slot + 2, me - 2).wait_send())
                to_device(index, origin, slot + 3, partner).wait_send()


def relay_gather(arrays, axes, req_total):
    lines = req_total // 2
    count = len(arrays)
    shapes = []
    for array, axis in zip(arrays, axes):
        if axis == 0:
            shape = (req_total,) + array.shape
        else:
            shape = (array.shape[0], req_total * array.shape[1])
        shapes.append(jax.ShapeDtypeStruct(shape, array.dtype))
    return pl.pallas_call(
        functools.partial(relay_kernel, lines, tuple(axes)),
        out_shape=shapes,
        in_specs=[pl.BlockSpec(memory_space=pl.ANY)] * count,
        out_specs=[pl.BlockSpec(memory_space=pl.ANY)] * count,
        scratch_shapes=[
            pltpu.SemaphoreType.DMA((count, 3 + 4 * (lines - 1))),
            pltpu.SemaphoreType.DMA((count, req_total)),
            pltpu.SemaphoreType.DMA((count,)),
        ],
        compiler_params=pltpu.CompilerParams(collective_id=0, has_side_effects=True),
    )(*arrays)


def gather_all(arrays, axes, req_total):
    if req_total % 2 == 0 and req_total <= 16:
        gathered = relay_gather(arrays, axes, req_total)
    else:
        gathered = [
            lax.all_gather(array, "req", axis=axis, tiled=axis == 1)
            for array, axis in zip(arrays, axes)
        ]
    return [
        array.reshape((-1,) + array.shape[2:]) if axis == 0 else array
        for array, axis in zip(gathered, axes)
    ]


def project_kernel(
    attended, weight, residual, out, sent_far, sent_near, sent_across, got_far, got_near, got_across,
    send_sems, recv_sems,
):
    me = lax.axis_index("tp")
    near = me + 1 - 2 * lax.rem(me, 2)
    across = lax.rem(me + 2, 4)
    far = lax.rem(near + 2, 4)
    width = out.shape[1]
    chunks = sent_far.shape[0]
    rows = sent_far.shape[1]

    def product(chunk, target):
        columns = pl.ds(pl.multiple_of(target * width, width), width)
        return jnp.dot(
            attended[pl.ds(chunk * rows, rows), :],
            weight[:, columns],
            preferred_element_type=jnp.float32,
        )

    def copy(kind, sent, got, chunk, target):
        return pltpu.make_async_remote_copy(
            src_ref=sent.at[chunk],
            dst_ref=got.at[chunk],
            send_sem=send_sems.at[kind, chunk],
            recv_sem=recv_sems.at[kind, chunk],
            device_id={"tp": target},
            device_id_type=pl.DeviceIdType.MESH,
        )

    def far_copy(chunk):
        return copy(0, sent_far, got_far, chunk, near)

    def near_copy(chunk):
        return copy(1, sent_near, got_near, chunk, near)

    def across_copy(chunk):
        return copy(2, sent_across, got_across, chunk, across)

    barrier = pltpu.get_barrier_semaphore()
    for target in (near, across):
        pl.semaphore_signal(
            barrier, inc=1, device_id={"tp": target}, device_id_type=pl.DeviceIdType.MESH
        )
    pl.semaphore_wait(barrier, 2)
    for chunk in range(chunks):
        sent_far[chunk] = product(chunk, far).astype(sent_far.dtype)
        far_copy(chunk).start()
    for chunk in range(chunks):
        mine = product(chunk, across)
        far_copy(chunk).wait_recv()
        sent_across[chunk] = (mine + got_far[chunk].astype(jnp.float32)).astype(sent_across.dtype)
        across_copy(chunk).start()
    for chunk in range(chunks):
        sent_near[chunk] = product(chunk, near).astype(sent_near.dtype)
        near_copy(chunk).start()
    for chunk in range(chunks):
        span = pl.ds(chunk * rows, rows)
        total = product(chunk, me) + residual[span, :].astype(jnp.float32)
        near_copy(chunk).wait_recv()
        total = total + got_near[chunk].astype(jnp.float32)
        across_copy(chunk).wait_recv()
        out[span, :] = (total + got_across[chunk].astype(jnp.float32)).astype(out.dtype)
    for chunk in range(chunks):
        far_copy(chunk).wait_send()
        across_copy(chunk).wait_send()
        near_copy(chunk).wait_send()


def project_and_scatter(attended, weight, residual):
    row_total = attended.shape[0]
    width = residual.shape[1]
    chunks = 4
    piece = pltpu.VMEM((chunks, row_total // chunks, width), jnp.bfloat16)
    return pl.pallas_call(
        project_kernel,
        out_shape=jax.ShapeDtypeStruct(residual.shape, residual.dtype),
        in_specs=[pl.BlockSpec(memory_space=pltpu.VMEM)] * 3,
        out_specs=pl.BlockSpec(memory_space=pltpu.VMEM),
        scratch_shapes=[piece] * 6
        + [pltpu.SemaphoreType.DMA((3, chunks)), pltpu.SemaphoreType.DMA((3, chunks))],
        compiler_params=pltpu.CompilerParams(
            collective_id=1, has_side_effects=True, vmem_limit_bytes=32 * 1024 * 1024
        ),
    )(attended, weight, residual)


def active_rows(stored, active_slots):
    slot_total = stored.shape[0]
    own = (active_slots // slot_total) == lax.axis_index("req")
    rows = jnp.where(
        own[:, None, None],
        jnp.take(stored, active_slots % slot_total, axis=0),
        jnp.zeros((), stored.dtype),
    )
    return lax.psum(rows, "req").reshape(-1, stored.shape[2])


def positions_of(segment):
    ordinal = jnp.arange(segment.shape[0], dtype=jnp.int32)
    starts = jnp.concatenate([jnp.ones((1,), jnp.bool_), segment[1:] != segment[:-1]])
    segment_start = lax.cummax(jnp.where(starts, ordinal, jnp.zeros_like(ordinal)), axis=0)
    return ordinal - segment_start


def apply_rotation(values, token_positions):
    half_dim = HEAD_WIDTH // 2
    frequency = rope_base ** (-(jnp.arange(half_dim, dtype=jnp.float32) * 2.0 / HEAD_WIDTH))
    angles = token_positions.astype(jnp.float32)[:, None] * frequency[None, :]
    cosine = jnp.cos(angles)[:, None, :]
    sine_part = jnp.sin(angles)[:, None, :]
    first_half = values[..., :half_dim]
    second_half = values[..., half_dim:]
    return jnp.concatenate(
        [
            first_half * cosine - second_half * sine_part,
            second_half * cosine + first_half * sine_part,
        ],
        axis=-1,
    )


def attend(query_per_head, key_heads, value_per_head, segment):
    scores = (
        jnp.einsum("qhd,khd->hqk", query_per_head, key_heads, preferred_element_type=jnp.float32)
        * 0.125
    )
    ordinal = jnp.arange(segment.shape[0], dtype=jnp.int32)
    allowed = (segment[:, None] == segment[None, :]) & (ordinal[None, :] <= ordinal[:, None])
    scores = jnp.where(allowed[None], scores, jnp.float32(-1e30))
    row_peak = jnp.max(scores, axis=-1, keepdims=True)
    exponent = jnp.where(allowed[None], jnp.exp(scores - row_peak), jnp.float32(0.0))
    weights = (exponent / jnp.sum(exponent, axis=-1, keepdims=True)).astype(jnp.bfloat16)
    return jnp.einsum(
        "hqk,khd->qhd", weights, value_per_head, preferred_element_type=jnp.float32
    ).astype(jnp.bfloat16)


def local(
    tokens,
    token_request_number,
    request_adapter_position,
    adapters_in_use,
    adapter_storage_slot,
    input_norm_gain,
    query_weight,
    key_weight,
    value_weight,
    output_weight,
    adapter_down_weight,
    adapter_up_weight,
):
    row_total, model_width = tokens.shape
    local_width = query_weight.shape[1]
    reduced_rows = adapter_down_weight.shape[2]
    slot_total = adapter_down_weight.shape[0]
    segment = token_request_number[0]
    request_adapters = request_adapter_position[0]
    tp_total = lax.axis_size("tp")
    req_total = lax.axis_size("req")
    part_rows = reduced_rows // tp_total
    share = 2 * part_rows
    down_part = lax.dynamic_slice_in_dim(
        adapter_down_weight, lax.axis_index("tp") * part_rows, part_rows, 2
    ).reshape(slot_total, share, model_width)
    up_part = adapter_up_weight.reshape(slot_total, 2 * reduced_rows, local_width)
    active_slots = jnp.take(adapter_storage_slot, adapters_in_use, axis=0)
    arrays = [query_weight, key_weight, value_weight, output_weight]
    axes = [0, 0, 0, 1]
    if slot_total * req_total <= 2 * active_slots.shape[0]:
        adapter_parts = [
            down_part.reshape(slot_total * share, model_width),
            up_part.reshape(slot_total * 2 * reduced_rows, local_width),
        ]
        down_all, up_all, query_full, key_full, value_full, output_full = gather_all(
            adapter_parts + arrays, [0, 0] + axes, req_total
        )
        request_places = active_slots[request_adapters]
    else:
        down_all = active_rows(down_part, active_slots)
        up_all = active_rows(up_part, active_slots)
        query_full, key_full, value_full, output_full = gather_all(arrays, axes, req_total)
        request_places = request_adapters
    place_total = down_all.shape[0] // share
    floats = tokens.astype(jnp.float32)
    normed = (
        floats
        * lax.rsqrt(jnp.mean(floats * floats, axis=-1, keepdims=True) + norm_eps)
        * input_norm_gain.astype(jnp.float32)
    ).astype(jnp.bfloat16)
    query_plain = jnp.dot(
        normed,
        query_full,
        preferred_element_type=jnp.float32,
    )
    key_base = jnp.dot(
        normed,
        key_full,
        preferred_element_type=jnp.float32,
    )
    value_plain = jnp.dot(
        normed,
        value_full,
        preferred_element_type=jnp.float32,
    )
    request_total = request_adapters.shape[0]
    member = segment[:, None] == jnp.arange(request_total, dtype=jnp.int32)[None, :]
    token_place = jnp.sum(
        jnp.where(member, request_places[None, :], jnp.zeros_like(request_places)[None, :]),
        axis=1,
    )
    shrunk_all = lax.dot_general(
        normed,
        down_all,
        (((1,), (1,)), ((), ())),
        preferred_element_type=jnp.float32,
    ).astype(jnp.bfloat16)
    column = jnp.arange(place_total * share, dtype=jnp.int32)
    kept = jnp.where(
        token_place[:, None] == (column // share)[None, :], shrunk_all, jnp.zeros((), jnp.bfloat16)
    )
    fold = (column % share)[:, None] == jnp.arange(share, dtype=jnp.int32)[None, :]
    shrunk_part = jnp.dot(
        kept, fold.astype(jnp.bfloat16), preferred_element_type=jnp.float32
    ).astype(jnp.bfloat16)
    shrunk = lax.all_gather(shrunk_part, "tp", axis=1, tiled=True)
    source = jnp.arange(tp_total * share, dtype=jnp.int32)
    source_kind = (source % share) // part_rows
    source_rank = (source // share) * part_rows + source % part_rows
    target = jnp.arange(place_total * reduced_rows, dtype=jnp.int32)
    mine = token_place[:, None] == (target // reduced_rows)[None, :]
    up_all = up_all.reshape(place_total, 2, reduced_rows, local_width)

    def change_of(kind):
        spread_map = (source_kind == kind)[:, None] & (
            source_rank[:, None] == (target % reduced_rows)[None, :]
        )
        spread = jnp.dot(
            shrunk, spread_map.astype(jnp.bfloat16), preferred_element_type=jnp.float32
        ).astype(jnp.bfloat16)
        spread = jnp.where(mine, spread, jnp.zeros((), jnp.bfloat16))
        return jnp.dot(
            spread,
            up_all[:, kind].reshape(place_total * reduced_rows, local_width),
            preferred_element_type=jnp.float32,
        )

    query_change = change_of(0)
    value_change = change_of(1)
    head_total = local_width // HEAD_WIDTH
    token_positions = positions_of(segment)
    query_per_head = apply_rotation(
        (query_plain + adapter_scale * query_change).reshape(row_total, head_total, HEAD_WIDTH),
        token_positions,
    ).astype(jnp.bfloat16)
    key_heads = apply_rotation(
        key_base.reshape(row_total, head_total, HEAD_WIDTH), token_positions
    ).astype(jnp.bfloat16)
    value_per_head = (
        (value_plain + adapter_scale * value_change)
        .astype(jnp.bfloat16)
        .reshape(row_total, head_total, HEAD_WIDTH)
    )
    attended = attend(query_per_head, key_heads, value_per_head, segment).reshape(
        row_total, local_width
    )
    share_width = model_width // tp_total
    residual_part = lax.dynamic_slice_in_dim(
        tokens, lax.axis_index("tp") * share_width, share_width, 1
    )
    if tp_total == 4:
        return project_and_scatter(attended, output_full, residual_part)
    partial_out = jnp.dot(attended, output_full, preferred_element_type=jnp.float32)
    summed = lax.psum_scatter(
        partial_out.astype(jnp.bfloat16), "tp", scatter_dimension=1, tiled=True
    ).astype(jnp.float32)
    return (summed + residual_part.astype(jnp.float32)).astype(jnp.bfloat16)


def solution(mesh):
    in_specs = (
        P("req", None),
        P("req", None),
        P("req", None),
        P(),
        P(),
        P(),
        P("req", "tp"),
        P("req", "tp"),
        P("req", "tp"),
        P("tp", "req"),
        P("req", None, None, None),
        P("req", None, None, "tp"),
    )
    out_specs = P("req", "tp")
    return jax.shard_map(local, mesh=mesh, in_specs=in_specs, out_specs=out_specs, check_vma=False)
```

```python
import functools

import jax
import jax.numpy as jnp
from jax import lax
from jax.experimental import pallas as pl
from jax.experimental.pallas import tpu as pltpu
from jax.sharding import PartitionSpec as P

HEAD_WIDTH = 64


norm_eps = 1e-05
rope_base = 130000.0
adapter_scale = 2.0


def relay_kernel(lines, axes, early, tp_total, *refs):
    count = len(axes)
    sources = refs[:count]
    normed, mask, fold = refs[count : count + 3]
    up_all, output_all, query_out, key_out, value_out, shrunk_out = refs[count + 3 : count + 9]
    down_all, query_all, key_all, value_all, shrunk_got = refs[count + 9 : count + 14]
    send_sems, recv_sems, local_sems, shrunk_send, shrunk_recv = refs[count + 14 :]
    gathered = (down_all, up_all, query_all, key_all, value_all, output_all)
    me = lax.axis_index("req")
    part = lax.axis_index("tp")
    line = lax.div(me, 2)
    side = lax.rem(me, 2)
    partner = 2 * line + 1 - side
    turn = 1 - 2 * side
    has_up = line < lines - 1
    has_down = line > 0

    def block(index, origin):
        if axes[index] == 0:
            return gathered[index].at[origin]
        width = sources[index].shape[1]
        return gathered[index].at[:, pl.ds(pl.multiple_of(origin * width, width), width)]

    def to_device(index, origin, slot, target):
        source = sources[index] if slot < 3 else block(index, origin)
        return pltpu.make_async_remote_copy(
            src_ref=source,
            dst_ref=block(index, origin),
            send_sem=send_sems.at[index, slot],
            recv_sem=recv_sems.at[index, origin],
            device_id={"req": target},
            device_id_type=pl.DeviceIdType.MESH,
        )

    def arrival(index, origin):
        to_device(index, origin, 3, partner).wait_recv()

    def own_copies(index, act):
        pl.when(has_up)(lambda: act(to_device(index, me, 0, me + 2)))
        pl.when(has_down)(lambda: act(to_device(index, me, 1, me - 2)))
        act(to_device(index, me, 2, partner))

    def pair_copies(index, act):
        pl.when(has_up)(lambda: act(to_device(index, partner, 3, me + 2)))
        pl.when(has_down)(lambda: act(to_device(index, partner, 4, me - 2)))

    def step_copies(index, step, act, receive):
        slot = 5 + 4 * (step - 1)

        for below, base, edge in ((True, slot, 2), (False, slot + 2, -2)):
            if below:
                origin = me - 2 * step
                held = line >= step
                onward = jnp.minimum(line - step, lines - 2 - line) >= 0
            else:
                origin = me + 2 * step
                held = line + step < lines
                onward = jnp.minimum(line - 1, lines - 1 - step - line) >= 0
            if index in early:
                if receive:

                    @pl.when(held)
                    def _():
                        arrival(index, origin)
                        arrival(index, origin + turn)

                @pl.when(onward)
                def _():
                    act(to_device(index, origin, base, me + edge))
                    act(to_device(index, origin + turn, base + 1, me + edge))

            else:

                @pl.when(held)
                def _():
                    if receive:
                        arrival(index, origin)
                    act(to_device(index, origin, base + 1, partner))

                @pl.when(onward)
                def _():
                    act(to_device(index, origin, base, me + edge))

    def start(copy):
        copy.start()

    def finish(copy):
        copy.wait_send()

    def local_copy(index):
        return pltpu.make_async_copy(sources[index], block(index, me), local_sems.at[index])

    def complete(index):
        if index not in early:
            for other in range(lines):
                arrival(index, 2 * other + 1 - side)
        local_copy(index).wait()

    def shrunk_copy(hop):
        return pltpu.make_async_remote_copy(
            src_ref=shrunk_out,
            dst_ref=shrunk_got.at[hop - 1],
            send_sem=shrunk_send.at[hop - 1],
            recv_sem=shrunk_recv.at[hop - 1],
            device_id={"tp": lax.rem(part + hop, tp_total)},
            device_id_type=pl.DeviceIdType.MESH,
        )

    barrier = pltpu.get_barrier_semaphore()

    def greet(device):
        pl.semaphore_signal(
            barrier, inc=1, device_id=device, device_id_type=pl.DeviceIdType.MESH
        )

    greet({"req": partner})
    pl.when(has_up)(lambda: greet({"req": me + 2}))
    pl.when(has_down)(lambda: greet({"req": me - 2}))
    for hop in range(1, tp_total):
        greet({"tp": lax.rem(part + hop, tp_total)})
    pl.semaphore_wait(barrier, tp_total + has_up.astype(jnp.int32) + has_down.astype(jnp.int32))

    for index in range(count):
        own_copies(index, start)
    for index in range(count):
        local_copy(index).start()
    for index in early:
        arrival(index, partner)
        pair_copies(index, start)
    for step in range(1, lines):
        for index in range(count):
            step_copies(index, step, start, True)

    rows = normed.shape[0] // 2

    complete(0)
    down = down_all[...].reshape(-1, down_all.shape[2])
    shrunk = lax.dot_general(
        normed[...], down, (((1,), (1,)), ((), ())), preferred_element_type=jnp.float32
    ).astype(jnp.bfloat16)
    shrunk_out[...] = jnp.dot(
        shrunk * mask[...], fold[...], preferred_element_type=jnp.float32
    ).astype(jnp.bfloat16)
    for hop in range(1, tp_total):
        shrunk_copy(hop).start()
    complete(1)
    for index, result in ((2, query_out), (3, key_out), (4, value_out)):
        complete(index)

        def one(piece, carry):
            span = pl.ds(pl.multiple_of(piece * rows, rows), rows)
            weight = gathered[index][...].reshape(-1, gathered[index].shape[2])
            result[span, :] = jnp.dot(
                normed[span, :], weight, preferred_element_type=jnp.float32
            )
            return carry

        lax.fori_loop(0, 2, one, 0)
    for hop in range(1, tp_total):
        shrunk_copy(hop).wait()
    total = shrunk_out[...]
    for hop in range(1, tp_total):
        total = total + shrunk_got[hop - 1]
    shrunk_out[...] = total
    complete(5)
    for index in range(count):
        own_copies(index, finish)
        if index in early:
            pair_copies(index, finish)
        for step in range(1, lines):
            step_copies(index, step, finish, False)


def relay_project(arrays, normed, mask, fold, req_total, tp_total):
    lines = req_total // 2
    axes = (0, 0, 0, 0, 0, 1)
    count = len(arrays)
    up, weight, output = arrays[1], arrays[2], arrays[5]
    row_total = normed.shape[0]
    base = jax.ShapeDtypeStruct((row_total, weight.shape[1]), jnp.float32)
    whole = pltpu.VMEM((req_total,) + weight.shape, weight.dtype)
    in_vmem = pl.BlockSpec(memory_space=pltpu.VMEM)
    anywhere = pl.BlockSpec(memory_space=pl.ANY)
    return pl.pallas_call(
        functools.partial(relay_kernel, lines, axes, (0, 1), tp_total),
        out_shape=[
            jax.ShapeDtypeStruct((req_total,) + up.shape, up.dtype),
            jax.ShapeDtypeStruct((output.shape[0], req_total * output.shape[1]), output.dtype),
            base,
            base,
            base,
            jax.ShapeDtypeStruct((row_total, fold.shape[1]), jnp.bfloat16),
        ],
        in_specs=[anywhere] * count + [in_vmem] * 3,
        out_specs=[anywhere] * 2 + [in_vmem] * 4,
        scratch_shapes=[
            pltpu.VMEM((req_total,) + arrays[0].shape, arrays[0].dtype),
            whole,
            whole,
            whole,
            pltpu.VMEM((tp_total - 1, row_total, fold.shape[1]), jnp.bfloat16),
            pltpu.SemaphoreType.DMA((count, 5 + 4 * (lines - 1))),
            pltpu.SemaphoreType.DMA((count, req_total)),
            pltpu.SemaphoreType.DMA((count,)),
            pltpu.SemaphoreType.DMA((tp_total - 1,)),
            pltpu.SemaphoreType.DMA((tp_total - 1,)),
        ],
        compiler_params=pltpu.CompilerParams(
            collective_id=0, has_side_effects=True, vmem_limit_bytes=40 * 1024 * 1024
        ),
    )(*arrays, normed, mask, fold)


def project_kernel(
    attended, weight, residual, out, sent_far, sent_near, sent_across, got_far, got_near, got_across,
    send_sems, recv_sems,
):
    me = lax.axis_index("tp")
    near = me + 1 - 2 * lax.rem(me, 2)
    across = lax.rem(me + 2, 4)
    far = lax.rem(near + 2, 4)
    width = out.shape[1]
    chunks = sent_far.shape[0]
    rows = sent_far.shape[1]

    def product(chunk, target):
        columns = pl.ds(pl.multiple_of(target * width, width), width)
        return jnp.dot(
            attended[pl.ds(chunk * rows, rows), :],
            weight[:, columns],
            preferred_element_type=jnp.float32,
        )

    def copy(kind, sent, got, chunk, target):
        return pltpu.make_async_remote_copy(
            src_ref=sent.at[chunk],
            dst_ref=got.at[chunk],
            send_sem=send_sems.at[kind, chunk],
            recv_sem=recv_sems.at[kind, chunk],
            device_id={"tp": target},
            device_id_type=pl.DeviceIdType.MESH,
        )

    def far_copy(chunk):
        return copy(0, sent_far, got_far, chunk, near)

    def near_copy(chunk):
        return copy(1, sent_near, got_near, chunk, near)

    def across_copy(chunk):
        return copy(2, sent_across, got_across, chunk, across)

    barrier = pltpu.get_barrier_semaphore()
    for target in (near, across):
        pl.semaphore_signal(
            barrier, inc=1, device_id={"tp": target}, device_id_type=pl.DeviceIdType.MESH
        )
    pl.semaphore_wait(barrier, 2)
    for chunk in range(chunks):
        sent_far[chunk] = product(chunk, far).astype(sent_far.dtype)
        far_copy(chunk).start()
    for chunk in range(chunks):
        mine = product(chunk, across)
        far_copy(chunk).wait_recv()
        sent_across[chunk] = (mine + got_far[chunk].astype(jnp.float32)).astype(sent_across.dtype)
        across_copy(chunk).start()
    for chunk in range(chunks):
        sent_near[chunk] = product(chunk, near).astype(sent_near.dtype)
        near_copy(chunk).start()
    for chunk in range(chunks):
        span = pl.ds(chunk * rows, rows)
        total = product(chunk, me) + residual[span, :].astype(jnp.float32)
        near_copy(chunk).wait_recv()
        total = total + got_near[chunk].astype(jnp.float32)
        across_copy(chunk).wait_recv()
        out[span, :] = (total + got_across[chunk].astype(jnp.float32)).astype(out.dtype)
    for chunk in range(chunks):
        far_copy(chunk).wait_send()
        across_copy(chunk).wait_send()
        near_copy(chunk).wait_send()


def project_and_scatter(attended, weight, residual):
    row_total = attended.shape[0]
    width = residual.shape[1]
    chunks = 4
    piece = pltpu.VMEM((chunks, row_total // chunks, width), jnp.bfloat16)
    return pl.pallas_call(
        project_kernel,
        out_shape=jax.ShapeDtypeStruct(residual.shape, residual.dtype),
        in_specs=[pl.BlockSpec(memory_space=pltpu.VMEM)] * 3,
        out_specs=pl.BlockSpec(memory_space=pltpu.VMEM),
        scratch_shapes=[piece] * 6
        + [pltpu.SemaphoreType.DMA((3, chunks)), pltpu.SemaphoreType.DMA((3, chunks))],
        compiler_params=pltpu.CompilerParams(
            collective_id=1, has_side_effects=True, vmem_limit_bytes=32 * 1024 * 1024
        ),
    )(attended, weight, residual)


def active_rows(stored, active_slots):
    slot_total = stored.shape[0]
    own = (active_slots // slot_total) == lax.axis_index("req")
    rows = jnp.where(
        own[:, None, None],
        jnp.take(stored, active_slots % slot_total, axis=0),
        jnp.zeros((), stored.dtype),
    )
    return lax.psum(rows, "req").reshape(-1, stored.shape[2])


def positions_of(segment):
    ordinal = jnp.arange(segment.shape[0], dtype=jnp.int32)
    starts = jnp.concatenate([jnp.ones((1,), jnp.bool_), segment[1:] != segment[:-1]])
    segment_start = lax.cummax(jnp.where(starts, ordinal, jnp.zeros_like(ordinal)), axis=0)
    return ordinal - segment_start


def apply_rotation(values, token_positions):
    half_dim = HEAD_WIDTH // 2
    frequency = rope_base ** (-(jnp.arange(half_dim, dtype=jnp.float32) * 2.0 / HEAD_WIDTH))
    angles = token_positions.astype(jnp.float32)[:, None] * frequency[None, :]
    cosine = jnp.cos(angles)[:, None, :]
    sine_part = jnp.sin(angles)[:, None, :]
    first_half = values[..., :half_dim]
    second_half = values[..., half_dim:]
    return jnp.concatenate(
        [
            first_half * cosine - second_half * sine_part,
            second_half * cosine + first_half * sine_part,
        ],
        axis=-1,
    )


def attend(query_per_head, key_heads, value_per_head, segment):
    scores = (
        jnp.einsum("qhd,khd->hqk", query_per_head, key_heads, preferred_element_type=jnp.float32)
        * 0.125
    )
    ordinal = jnp.arange(segment.shape[0], dtype=jnp.int32)
    allowed = (segment[:, None] == segment[None, :]) & (ordinal[None, :] <= ordinal[:, None])
    scores = jnp.where(allowed[None], scores, jnp.float32(-1e30))
    row_peak = jnp.max(scores, axis=-1, keepdims=True)
    exponent = jnp.where(allowed[None], jnp.exp(scores - row_peak), jnp.float32(0.0))
    weights = (exponent / jnp.sum(exponent, axis=-1, keepdims=True)).astype(jnp.bfloat16)
    return jnp.einsum(
        "hqk,khd->qhd", weights, value_per_head, preferred_element_type=jnp.float32
    ).astype(jnp.bfloat16)


def local(
    tokens,
    token_request_number,
    request_adapter_position,
    adapters_in_use,
    adapter_storage_slot,
    input_norm_gain,
    query_weight,
    key_weight,
    value_weight,
    output_weight,
    adapter_down_weight,
    adapter_up_weight,
):
    row_total, model_width = tokens.shape
    local_width = query_weight.shape[1]
    reduced_rows = adapter_down_weight.shape[2]
    slot_total = adapter_down_weight.shape[0]
    segment = token_request_number[0]
    request_adapters = request_adapter_position[0]
    tp_total = lax.axis_size("tp")
    req_total = lax.axis_size("req")
    part_rows = reduced_rows // tp_total
    share = 2 * part_rows
    down_part = lax.dynamic_slice_in_dim(
        adapter_down_weight, lax.axis_index("tp") * part_rows, part_rows, 2
    ).reshape(slot_total, share, model_width)
    up_part = adapter_up_weight.reshape(slot_total, 2 * reduced_rows, local_width)
    active_slots = jnp.take(adapter_storage_slot, adapters_in_use, axis=0)
    floats = tokens.astype(jnp.float32)
    normed = (
        floats
        * lax.rsqrt(jnp.mean(floats * floats, axis=-1, keepdims=True) + norm_eps)
        * input_norm_gain.astype(jnp.float32)
    ).astype(jnp.bfloat16)
    relayed = req_total % 2 == 0 and req_total <= 16
    relayed = relayed and slot_total * req_total <= 2 * active_slots.shape[0]
    if relayed:
        place_total = slot_total * req_total
        request_places = active_slots[request_adapters]
    else:
        place_total = active_slots.shape[0]
        request_places = request_adapters
    member = segment[:, None] == jnp.arange(request_adapters.shape[0], dtype=jnp.int32)[None, :]
    token_place = jnp.sum(
        jnp.where(member, request_places[None, :], jnp.zeros_like(request_places)[None, :]),
        axis=1,
    )
    column = jnp.arange(place_total * share, dtype=jnp.int32)
    mask = (token_place[:, None] == (column // share)[None, :]).astype(jnp.bfloat16)
    lanes = max(128, tp_total * share)
    fold = (lax.axis_index("tp") * share + column % share)[:, None] == jnp.arange(
        lanes, dtype=jnp.int32
    )[None, :]
    fold = fold.astype(jnp.bfloat16)
    if relayed:
        arrays = [
            down_part.reshape(slot_total * share, model_width),
            up_part.reshape(slot_total * 2 * reduced_rows, local_width),
            query_weight,
            key_weight,
            value_weight,
            output_weight,
        ]
        up_all, output_full, query_plain, key_base, value_plain, shrunk = relay_project(
            arrays, normed, mask, fold, req_total, tp_total
        )
    else:
        down_all = active_rows(down_part, active_slots)
        up_all = active_rows(up_part, active_slots)
        output_full = lax.all_gather(output_weight, "req", axis=1, tiled=True)
        query_plain, key_base, value_plain = [
            jnp.dot(
                normed,
                lax.all_gather(weight, "req", axis=0, tiled=True),
                preferred_element_type=jnp.float32,
            )
            for weight in (query_weight, key_weight, value_weight)
        ]
        shrunk_all = lax.dot_general(
            normed, down_all, (((1,), (1,)), ((), ())), preferred_element_type=jnp.float32
        ).astype(jnp.bfloat16)
        shrunk = lax.psum(
            jnp.dot(shrunk_all * mask, fold, preferred_element_type=jnp.float32), "tp"
        ).astype(jnp.bfloat16)
    shrunk = shrunk[:, : tp_total * share]
    source = jnp.arange(tp_total * share, dtype=jnp.int32)
    source_kind = (source % share) // part_rows
    source_rank = (source // share) * part_rows + source % part_rows
    target = jnp.arange(place_total * reduced_rows, dtype=jnp.int32)
    mine = token_place[:, None] == (target // reduced_rows)[None, :]
    up_all = up_all.reshape(place_total, 2, reduced_rows, local_width)

    def change_of(kind):
        spread_map = (source_kind == kind)[:, None] & (
            source_rank[:, None] == (target % reduced_rows)[None, :]
        )
        spread = jnp.dot(
            shrunk, spread_map.astype(jnp.bfloat16), preferred_element_type=jnp.float32
        ).astype(jnp.bfloat16)
        spread = jnp.where(mine, spread, jnp.zeros((), jnp.bfloat16))
        return jnp.dot(
            spread,
            up_all[:, kind].reshape(place_total * reduced_rows, local_width),
            preferred_element_type=jnp.float32,
        )

    query_change = change_of(0)
    value_change = change_of(1)
    head_total = local_width // HEAD_WIDTH
    token_positions = positions_of(segment)
    query_per_head = apply_rotation(
        (query_plain + adapter_scale * query_change).reshape(row_total, head_total, HEAD_WIDTH),
        token_positions,
    ).astype(jnp.bfloat16)
    key_heads = apply_rotation(
        key_base.reshape(row_total, head_total, HEAD_WIDTH), token_positions
    ).astype(jnp.bfloat16)
    value_per_head = (
        (value_plain + adapter_scale * value_change)
        .astype(jnp.bfloat16)
        .reshape(row_total, head_total, HEAD_WIDTH)
    )
    attended = attend(query_per_head, key_heads, value_per_head, segment).reshape(
        row_total, local_width
    )
    share_width = model_width // tp_total
    residual_part = lax.dynamic_slice_in_dim(
        tokens, lax.axis_index("tp") * share_width, share_width, 1
    )
    if tp_total == 4:
        return project_and_scatter(attended, output_full, residual_part)
    partial_out = jnp.dot(attended, output_full, preferred_element_type=jnp.float32)
    summed = lax.psum_scatter(
        partial_out.astype(jnp.bfloat16), "tp", scatter_dimension=1, tiled=True
    ).astype(jnp.float32)
    return (summed + residual_part.astype(jnp.float32)).astype(jnp.bfloat16)


def solution(mesh):
    in_specs = (
        P("req", None),
        P("req", None),
        P("req", None),
        P(),
        P(),
        P(),
        P("req", "tp"),
        P("req", "tp"),
        P("req", "tp"),
        P("tp", "req"),
        P("req", None, None, None),
        P("req", None, None, "tp"),
    )
    out_specs = P("req", "tp")
    return jax.shard_map(local, mesh=mesh, in_specs=in_specs, out_specs=out_specs, check_vma=False)
```

```python
import functools

import jax
import jax.numpy as jnp
from jax import lax
from jax.experimental import pallas as pl
from jax.experimental.pallas import tpu as pltpu
from jax.sharding import PartitionSpec as P

HEAD_WIDTH = 64


norm_eps = 1e-05
rope_base = 130000.0
adapter_scale = 2.0


def relay_kernel(lines, axes, early, tp_total, *refs):
    count = len(axes)
    sources = refs[:count]
    tokens, gain, mask, fold = refs[count : count + 4]
    up_all, output_all, query_out, key_out, value_out, shrunk_out = refs[count + 4 : count + 10]
    down_all, query_all, key_all, value_all, shrunk_got, normed = refs[count + 10 : count + 16]
    send_sems, recv_sems, local_sems, shrunk_send, shrunk_recv = refs[count + 16 :]
    gathered = (down_all, up_all, query_all, key_all, value_all, output_all)
    me = lax.axis_index("req")
    part = lax.axis_index("tp")
    line = lax.div(me, 2)
    side = lax.rem(me, 2)
    partner = 2 * line + 1 - side
    turn = 1 - 2 * side
    has_up = line < lines - 1
    has_down = line > 0

    def block(index, origin):
        if axes[index] == 0:
            return gathered[index].at[origin]
        width = sources[index].shape[1]
        return gathered[index].at[:, pl.ds(pl.multiple_of(origin * width, width), width)]

    def to_device(index, origin, slot, target):
        source = sources[index] if slot < 3 else block(index, origin)
        return pltpu.make_async_remote_copy(
            src_ref=source,
            dst_ref=block(index, origin),
            send_sem=send_sems.at[index, slot],
            recv_sem=recv_sems.at[index, origin],
            device_id={"req": target},
            device_id_type=pl.DeviceIdType.MESH,
        )

    def arrival(index, origin):
        to_device(index, origin, 3, partner).wait_recv()

    def own_copies(index, act):
        pl.when(has_up)(lambda: act(to_device(index, me, 0, me + 2)))
        pl.when(has_down)(lambda: act(to_device(index, me, 1, me - 2)))
        act(to_device(index, me, 2, partner))

    def pair_copies(index, act):
        pl.when(has_up)(lambda: act(to_device(index, partner, 3, me + 2)))
        pl.when(has_down)(lambda: act(to_device(index, partner, 4, me - 2)))

    def step_copies(index, step, act, receive):
        slot = 5 + 4 * (step - 1)

        for below, base, edge in ((True, slot, 2), (False, slot + 2, -2)):
            if below:
                origin = me - 2 * step
                held = line >= step
                onward = jnp.minimum(line - step, lines - 2 - line) >= 0
            else:
                origin = me + 2 * step
                held = line + step < lines
                onward = jnp.minimum(line - 1, lines - 1 - step - line) >= 0
            if index in early:
                if receive:

                    @pl.when(held)
                    def _():
                        arrival(index, origin)
                        arrival(index, origin + turn)

                @pl.when(onward)
                def _():
                    act(to_device(index, origin, base, me + edge))
                    act(to_device(index, origin + turn, base + 1, me + edge))

            else:

                @pl.when(held)
                def _():
                    if receive:
                        arrival(index, origin)
                    act(to_device(index, origin, base + 1, partner))

                @pl.when(onward)
                def _():
                    act(to_device(index, origin, base, me + edge))

    def start(copy):
        copy.start()

    def finish(copy):
        copy.wait_send()

    def local_copy(index):
        return pltpu.make_async_copy(sources[index], block(index, me), local_sems.at[index])

    def complete(index):
        if index not in early:
            for other in range(lines):
                arrival(index, 2 * other + 1 - side)
        local_copy(index).wait()

    def shrunk_copy(hop):
        return pltpu.make_async_remote_copy(
            src_ref=shrunk_out,
            dst_ref=shrunk_got.at[hop - 1],
            send_sem=shrunk_send.at[hop - 1],
            recv_sem=shrunk_recv.at[hop - 1],
            device_id={"tp": lax.rem(part + hop, tp_total)},
            device_id_type=pl.DeviceIdType.MESH,
        )

    barrier = pltpu.get_barrier_semaphore()

    def greet(device):
        pl.semaphore_signal(
            barrier, inc=1, device_id=device, device_id_type=pl.DeviceIdType.MESH
        )

    greet({"req": partner})
    pl.when(has_up)(lambda: greet({"req": me + 2}))
    pl.when(has_down)(lambda: greet({"req": me - 2}))
    for hop in range(1, tp_total):
        greet({"tp": lax.rem(part + hop, tp_total)})
    pl.semaphore_wait(barrier, tp_total + has_up.astype(jnp.int32) + has_down.astype(jnp.int32))

    for index in range(count):
        own_copies(index, start)
    for index in range(count):
        local_copy(index).start()
    norm_rows = normed.shape[0] // 8

    def normalise(piece, carry):
        span = pl.ds(pl.multiple_of(piece * norm_rows, norm_rows), norm_rows)
        floats = tokens[span, :].astype(jnp.float32)
        mean = jnp.mean(floats * floats, axis=-1, keepdims=True)
        normed[span, :] = (
            floats * lax.rsqrt(mean + norm_eps) * gain[...].astype(jnp.float32)
        ).astype(normed.dtype)
        return carry

    lax.fori_loop(0, 8, normalise, 0)
    for index in early:
        arrival(index, partner)
        pair_copies(index, start)
    for step in range(1, lines):
        for index in range(count):
            step_copies(index, step, start, True)

    rows = normed.shape[0] // 2

    complete(0)
    down = down_all[...].reshape(-1, down_all.shape[2])
    shrunk = lax.dot_general(
        normed[...], down, (((1,), (1,)), ((), ())), preferred_element_type=jnp.float32
    ).astype(jnp.bfloat16)
    shrunk_out[...] = jnp.dot(
        shrunk * mask[...], fold[...], preferred_element_type=jnp.float32
    ).astype(jnp.bfloat16)
    for hop in range(1, tp_total):
        shrunk_copy(hop).start()
    complete(1)
    for index, result in ((2, query_out), (3, key_out), (4, value_out)):
        complete(index)

        def one(piece, carry):
            span = pl.ds(pl.multiple_of(piece * rows, rows), rows)
            weight = gathered[index][...].reshape(-1, gathered[index].shape[2])
            result[span, :] = jnp.dot(
                normed[span, :], weight, preferred_element_type=jnp.float32
            )
            return carry

        lax.fori_loop(0, 2, one, 0)
    for hop in range(1, tp_total):
        shrunk_copy(hop).wait()
    total = shrunk_out[...]
    for hop in range(1, tp_total):
        total = total + shrunk_got[hop - 1]
    shrunk_out[...] = total
    complete(5)
    for index in range(count):
        own_copies(index, finish)
        if index in early:
            pair_copies(index, finish)
        for step in range(1, lines):
            step_copies(index, step, finish, False)


def relay_project(arrays, tokens, gain, mask, fold, req_total, tp_total):
    lines = req_total // 2
    axes = (0, 0, 0, 0, 0, 1)
    count = len(arrays)
    up, weight, output = arrays[1], arrays[2], arrays[5]
    row_total = tokens.shape[0]
    base = jax.ShapeDtypeStruct((row_total, weight.shape[1]), jnp.float32)
    whole = pltpu.VMEM((req_total,) + weight.shape, weight.dtype)
    in_vmem = pl.BlockSpec(memory_space=pltpu.VMEM)
    anywhere = pl.BlockSpec(memory_space=pl.ANY)
    return pl.pallas_call(
        functools.partial(relay_kernel, lines, axes, (0, 1), tp_total),
        out_shape=[
            jax.ShapeDtypeStruct((req_total,) + up.shape, up.dtype),
            jax.ShapeDtypeStruct((output.shape[0], req_total * output.shape[1]), output.dtype),
            base,
            base,
            base,
            jax.ShapeDtypeStruct((row_total, fold.shape[1]), jnp.bfloat16),
        ],
        in_specs=[pl.BlockSpec(memory_space=pltpu.HBM)] * count + [in_vmem] * 4,
        out_specs=[anywhere] * 2 + [in_vmem] * 4,
        scratch_shapes=[
            pltpu.VMEM((req_total,) + arrays[0].shape, arrays[0].dtype),
            whole,
            whole,
            whole,
            pltpu.VMEM((tp_total - 1, row_total, fold.shape[1]), jnp.bfloat16),
            pltpu.VMEM(tokens.shape, jnp.bfloat16),
            pltpu.SemaphoreType.DMA((count, 5 + 4 * (lines - 1))),
            pltpu.SemaphoreType.DMA((count, req_total)),
            pltpu.SemaphoreType.DMA((count,)),
            pltpu.SemaphoreType.DMA((tp_total - 1,)),
            pltpu.SemaphoreType.DMA((tp_total - 1,)),
        ],
        compiler_params=pltpu.CompilerParams(
            collective_id=0, has_side_effects=True, vmem_limit_bytes=40 * 1024 * 1024
        ),
    )(*arrays, tokens, gain, mask, fold)


def project_kernel(
    attended, weight, residual, out, sent_far, sent_near, sent_across, got_far, got_near, got_across,
    send_sems, recv_sems,
):
    me = lax.axis_index("tp")
    near = me + 1 - 2 * lax.rem(me, 2)
    across = lax.rem(me + 2, 4)
    far = lax.rem(near + 2, 4)
    width = out.shape[1]
    chunks = sent_far.shape[0]
    rows = sent_far.shape[1]

    def product(chunk, target):
        columns = pl.ds(pl.multiple_of(target * width, width), width)
        return jnp.dot(
            attended[pl.ds(chunk * rows, rows), :],
            weight[:, columns],
            preferred_element_type=jnp.float32,
        )

    def copy(kind, sent, got, chunk, target):
        return pltpu.make_async_remote_copy(
            src_ref=sent.at[chunk],
            dst_ref=got.at[chunk],
            send_sem=send_sems.at[kind, chunk],
            recv_sem=recv_sems.at[kind, chunk],
            device_id={"tp": target},
            device_id_type=pl.DeviceIdType.MESH,
        )

    def far_copy(chunk):
        return copy(0, sent_far, got_far, chunk, near)

    def near_copy(chunk):
        return copy(1, sent_near, got_near, chunk, near)

    def across_copy(chunk):
        return copy(2, sent_across, got_across, chunk, across)

    barrier = pltpu.get_barrier_semaphore()
    for target in (near, across):
        pl.semaphore_signal(
            barrier, inc=1, device_id={"tp": target}, device_id_type=pl.DeviceIdType.MESH
        )
    pl.semaphore_wait(barrier, 2)
    for chunk in range(chunks):
        sent_far[chunk] = product(chunk, far).astype(sent_far.dtype)
        far_copy(chunk).start()
    for chunk in range(chunks):
        mine = product(chunk, across)
        far_copy(chunk).wait_recv()
        sent_across[chunk] = (mine + got_far[chunk].astype(jnp.float32)).astype(sent_across.dtype)
        across_copy(chunk).start()
    for chunk in range(chunks):
        sent_near[chunk] = product(chunk, near).astype(sent_near.dtype)
        near_copy(chunk).start()
    for chunk in range(chunks):
        span = pl.ds(chunk * rows, rows)
        total = product(chunk, me) + residual[span, :].astype(jnp.float32)
        near_copy(chunk).wait_recv()
        total = total + got_near[chunk].astype(jnp.float32)
        across_copy(chunk).wait_recv()
        out[span, :] = (total + got_across[chunk].astype(jnp.float32)).astype(out.dtype)
    for chunk in range(chunks):
        far_copy(chunk).wait_send()
        across_copy(chunk).wait_send()
        near_copy(chunk).wait_send()


def project_and_scatter(attended, weight, residual):
    row_total = attended.shape[0]
    width = residual.shape[1]
    chunks = 4
    piece = pltpu.VMEM((chunks, row_total // chunks, width), jnp.bfloat16)
    return pl.pallas_call(
        project_kernel,
        out_shape=jax.ShapeDtypeStruct(residual.shape, residual.dtype),
        in_specs=[pl.BlockSpec(memory_space=pltpu.VMEM)] * 3,
        out_specs=pl.BlockSpec(memory_space=pltpu.VMEM),
        scratch_shapes=[piece] * 6
        + [pltpu.SemaphoreType.DMA((3, chunks)), pltpu.SemaphoreType.DMA((3, chunks))],
        compiler_params=pltpu.CompilerParams(
            collective_id=1, has_side_effects=True, vmem_limit_bytes=32 * 1024 * 1024
        ),
    )(attended, weight, residual)


def active_rows(stored, active_slots):
    slot_total = stored.shape[0]
    own = (active_slots // slot_total) == lax.axis_index("req")
    rows = jnp.where(
        own[:, None, None],
        jnp.take(stored, active_slots % slot_total, axis=0),
        jnp.zeros((), stored.dtype),
    )
    return lax.psum(rows, "req").reshape(-1, stored.shape[2])


def positions_of(segment):
    ordinal = jnp.arange(segment.shape[0], dtype=jnp.int32)
    starts = jnp.concatenate([jnp.ones((1,), jnp.bool_), segment[1:] != segment[:-1]])
    segment_start = lax.cummax(jnp.where(starts, ordinal, jnp.zeros_like(ordinal)), axis=0)
    return ordinal - segment_start


def apply_rotation(values, token_positions):
    half_dim = HEAD_WIDTH // 2
    frequency = rope_base ** (-(jnp.arange(half_dim, dtype=jnp.float32) * 2.0 / HEAD_WIDTH))
    angles = token_positions.astype(jnp.float32)[:, None] * frequency[None, :]
    cosine = jnp.cos(angles)[:, None, :]
    sine_part = jnp.sin(angles)[:, None, :]
    first_half = values[..., :half_dim]
    second_half = values[..., half_dim:]
    return jnp.concatenate(
        [
            first_half * cosine - second_half * sine_part,
            second_half * cosine + first_half * sine_part,
        ],
        axis=-1,
    )


def attend(query_per_head, key_heads, value_per_head, segment):
    scores = (
        jnp.einsum("qhd,khd->hqk", query_per_head, key_heads, preferred_element_type=jnp.float32)
        * 0.125
    )
    ordinal = jnp.arange(segment.shape[0], dtype=jnp.int32)
    allowed = (segment[:, None] == segment[None, :]) & (ordinal[None, :] <= ordinal[:, None])
    scores = jnp.where(allowed[None], scores, jnp.float32(-1e30))
    row_peak = jnp.max(scores, axis=-1, keepdims=True)
    exponent = jnp.where(allowed[None], jnp.exp(scores - row_peak), jnp.float32(0.0))
    weights = (exponent / jnp.sum(exponent, axis=-1, keepdims=True)).astype(jnp.bfloat16)
    return jnp.einsum(
        "hqk,khd->qhd", weights, value_per_head, preferred_element_type=jnp.float32
    ).astype(jnp.bfloat16)


def local(
    tokens,
    token_request_number,
    request_adapter_position,
    adapters_in_use,
    adapter_storage_slot,
    input_norm_gain,
    query_weight,
    key_weight,
    value_weight,
    output_weight,
    adapter_down_weight,
    adapter_up_weight,
):
    row_total, model_width = tokens.shape
    local_width = query_weight.shape[1]
    reduced_rows = adapter_down_weight.shape[2]
    slot_total = adapter_down_weight.shape[0]
    segment = token_request_number[0]
    request_adapters = request_adapter_position[0]
    tp_total = lax.axis_size("tp")
    req_total = lax.axis_size("req")
    part_rows = reduced_rows // tp_total
    share = 2 * part_rows
    down_part = lax.dynamic_slice_in_dim(
        adapter_down_weight, lax.axis_index("tp") * part_rows, part_rows, 2
    ).reshape(slot_total, share, model_width)
    up_part = adapter_up_weight.reshape(slot_total, 2 * reduced_rows, local_width)
    active_slots = jnp.take(adapter_storage_slot, adapters_in_use, axis=0)
    relayed = req_total % 2 == 0 and req_total <= 16
    relayed = relayed and slot_total * req_total <= 2 * active_slots.shape[0]
    if relayed:
        place_total = slot_total * req_total
        request_places = active_slots[request_adapters]
    else:
        place_total = active_slots.shape[0]
        request_places = request_adapters
    member = segment[:, None] == jnp.arange(request_adapters.shape[0], dtype=jnp.int32)[None, :]
    token_place = jnp.sum(
        jnp.where(member, request_places[None, :], jnp.zeros_like(request_places)[None, :]),
        axis=1,
    )
    column = jnp.arange(place_total * share, dtype=jnp.int32)
    mask = (token_place[:, None] == (column // share)[None, :]).astype(jnp.bfloat16)
    lanes = max(128, tp_total * share)
    fold = (lax.axis_index("tp") * share + column % share)[:, None] == jnp.arange(
        lanes, dtype=jnp.int32
    )[None, :]
    fold = fold.astype(jnp.bfloat16)
    if relayed:
        arrays = [
            down_part.reshape(slot_total * share, model_width),
            up_part.reshape(slot_total * 2 * reduced_rows, local_width),
            query_weight,
            key_weight,
            value_weight,
            output_weight,
        ]
        up_all, output_full, query_plain, key_base, value_plain, shrunk = relay_project(
            arrays, tokens, input_norm_gain[None, :], mask, fold, req_total, tp_total
        )
    else:
        floats = tokens.astype(jnp.float32)
        normed = (
            floats
            * lax.rsqrt(jnp.mean(floats * floats, axis=-1, keepdims=True) + norm_eps)
            * input_norm_gain.astype(jnp.float32)
        ).astype(jnp.bfloat16)
        down_all = active_rows(down_part, active_slots)
        up_all = active_rows(up_part, active_slots)
        output_full = lax.all_gather(output_weight, "req", axis=1, tiled=True)
        query_plain, key_base, value_plain = [
            jnp.dot(
                normed,
                lax.all_gather(weight, "req", axis=0, tiled=True),
                preferred_element_type=jnp.float32,
            )
            for weight in (query_weight, key_weight, value_weight)
        ]
        shrunk_all = lax.dot_general(
            normed, down_all, (((1,), (1,)), ((), ())), preferred_element_type=jnp.float32
        ).astype(jnp.bfloat16)
        shrunk = lax.psum(
            jnp.dot(shrunk_all * mask, fold, preferred_element_type=jnp.float32), "tp"
        ).astype(jnp.bfloat16)
    shrunk = shrunk[:, : tp_total * share]
    source = jnp.arange(tp_total * share, dtype=jnp.int32)
    source_kind = (source % share) // part_rows
    source_rank = (source // share) * part_rows + source % part_rows
    target = jnp.arange(place_total * reduced_rows, dtype=jnp.int32)
    mine = token_place[:, None] == (target // reduced_rows)[None, :]
    up_all = up_all.reshape(place_total, 2, reduced_rows, local_width)

    def change_of(kind):
        spread_map = (source_kind == kind)[:, None] & (
            source_rank[:, None] == (target % reduced_rows)[None, :]
        )
        spread = jnp.dot(
            shrunk, spread_map.astype(jnp.bfloat16), preferred_element_type=jnp.float32
        ).astype(jnp.bfloat16)
        spread = jnp.where(mine, spread, jnp.zeros((), jnp.bfloat16))
        return jnp.dot(
            spread,
            up_all[:, kind].reshape(place_total * reduced_rows, local_width),
            preferred_element_type=jnp.float32,
        )

    query_change = change_of(0)
    value_change = change_of(1)
    head_total = local_width // HEAD_WIDTH
    token_positions = positions_of(segment)
    query_per_head = apply_rotation(
        (query_plain + adapter_scale * query_change).reshape(row_total, head_total, HEAD_WIDTH),
        token_positions,
    ).astype(jnp.bfloat16)
    key_heads = apply_rotation(
        key_base.reshape(row_total, head_total, HEAD_WIDTH), token_positions
    ).astype(jnp.bfloat16)
    value_per_head = (
        (value_plain + adapter_scale * value_change)
        .astype(jnp.bfloat16)
        .reshape(row_total, head_total, HEAD_WIDTH)
    )
    attended = attend(query_per_head, key_heads, value_per_head, segment).reshape(
        row_total, local_width
    )
    share_width = model_width // tp_total
    residual_part = lax.dynamic_slice_in_dim(
        tokens, lax.axis_index("tp") * share_width, share_width, 1
    )
    if tp_total == 4:
        return project_and_scatter(attended, output_full, residual_part)
    partial_out = jnp.dot(attended, output_full, preferred_element_type=jnp.float32)
    summed = lax.psum_scatter(
        partial_out.astype(jnp.bfloat16), "tp", scatter_dimension=1, tiled=True
    ).astype(jnp.float32)
    return (summed + residual_part.astype(jnp.float32)).astype(jnp.bfloat16)


def solution(mesh):
    in_specs = (
        P("req", None),
        P("req", None),
        P("req", None),
        P(),
        P(),
        P(),
        P("req", "tp"),
        P("req", "tp"),
        P("req", "tp"),
        P("tp", "req"),
        P("req", None, None, None),
        P("req", None, None, "tp"),
    )
    out_specs = P("req", "tp")
    return jax.shard_map(local, mesh=mesh, in_specs=in_specs, out_specs=out_specs, check_vma=False)
```

```python
import functools

import jax
import jax.numpy as jnp
from jax import lax
from jax.experimental import pallas as pl
from jax.experimental.pallas import tpu as pltpu
from jax.sharding import PartitionSpec as P

HEAD_WIDTH = 64


norm_eps = 1e-05
rope_base = 130000.0
adapter_scale = 2.0


def relay_kernel(lines, axes, early, tp_total, *refs):
    count = len(axes)
    sources = refs[:count]
    tokens, gain, mask, fold = refs[count : count + 4]
    up_all, output_all, query_out, key_out, value_out, shrunk_out = refs[count + 4 : count + 10]
    down_all, query_all, key_all, value_all, shrunk_got, normed = refs[count + 10 : count + 16]
    send_sems, recv_sems, local_sems, shrunk_send, shrunk_recv = refs[count + 16 :]
    gathered = (down_all, up_all, query_all, key_all, value_all, output_all)
    me = lax.axis_index("req")
    part = lax.axis_index("tp")
    line = lax.div(me, 2)
    side = lax.rem(me, 2)
    partner = 2 * line + 1 - side
    turn = 1 - 2 * side
    has_up = line < lines - 1
    has_down = line > 0

    def block(index, origin):
        if axes[index] == 0:
            return gathered[index].at[origin]
        width = sources[index].shape[1]
        return gathered[index].at[:, pl.ds(pl.multiple_of(origin * width, width), width)]

    def to_device(index, origin, slot, target):
        source = sources[index] if slot < 3 else block(index, origin)
        return pltpu.make_async_remote_copy(
            src_ref=source,
            dst_ref=block(index, origin),
            send_sem=send_sems.at[index, slot],
            recv_sem=recv_sems.at[index, origin],
            device_id={"req": target},
            device_id_type=pl.DeviceIdType.MESH,
        )

    def arrival(index, origin):
        to_device(index, origin, 3, partner).wait_recv()

    def own_copies(index, act):
        pl.when(has_up)(lambda: act(to_device(index, me, 0, me + 2)))
        pl.when(has_down)(lambda: act(to_device(index, me, 1, me - 2)))
        act(to_device(index, me, 2, partner))

    def pair_copies(index, act):
        pl.when(has_up)(lambda: act(to_device(index, partner, 3, me + 2)))
        pl.when(has_down)(lambda: act(to_device(index, partner, 4, me - 2)))

    def step_copies(index, step, act, receive):
        slot = 5 + 4 * (step - 1)

        for below, base, edge in ((True, slot, 2), (False, slot + 2, -2)):
            if below:
                origin = me - 2 * step
                held = line >= step
                onward = jnp.minimum(line - step, lines - 2 - line) >= 0
            else:
                origin = me + 2 * step
                held = line + step < lines
                onward = jnp.minimum(line - 1, lines - 1 - step - line) >= 0
            if index in early:
                if receive:

                    @pl.when(held)
                    def _():
                        arrival(index, origin)
                        arrival(index, origin + turn)

                @pl.when(onward)
                def _():
                    act(to_device(index, origin, base, me + edge))
                    act(to_device(index, origin + turn, base + 1, me + edge))

            else:

                @pl.when(held)
                def _():
                    if receive:
                        arrival(index, origin)
                    act(to_device(index, origin, base + 1, partner))

                @pl.when(onward)
                def _():
                    act(to_device(index, origin, base, me + edge))

    def start(copy):
        copy.start()

    def finish(copy):
        copy.wait_send()

    def local_copy(index):
        return pltpu.make_async_copy(sources[index], block(index, me), local_sems.at[index])

    def complete(index):
        if index not in early:
            for other in range(lines):
                arrival(index, 2 * other + 1 - side)
        local_copy(index).wait()

    def shrunk_copy(hop):
        return pltpu.make_async_remote_copy(
            src_ref=shrunk_out,
            dst_ref=shrunk_got.at[hop - 1],
            send_sem=shrunk_send.at[hop - 1],
            recv_sem=shrunk_recv.at[hop - 1],
            device_id={"tp": lax.rem(part + hop, tp_total)},
            device_id_type=pl.DeviceIdType.MESH,
        )

    barrier = pltpu.get_barrier_semaphore()

    def greet(device):
        pl.semaphore_signal(
            barrier, inc=1, device_id=device, device_id_type=pl.DeviceIdType.MESH
        )

    greet({"req": partner})
    pl.when(has_up)(lambda: greet({"req": me + 2}))
    pl.when(has_down)(lambda: greet({"req": me - 2}))
    for hop in range(1, tp_total):
        greet({"tp": lax.rem(part + hop, tp_total)})
    pl.semaphore_wait(barrier, tp_total + has_up.astype(jnp.int32) + has_down.astype(jnp.int32))

    for index in range(count):
        own_copies(index, start)
    for index in range(count):
        local_copy(index).start()
    norm_rows = normed.shape[0] // 8

    def normalise(piece, carry):
        span = pl.ds(pl.multiple_of(piece * norm_rows, norm_rows), norm_rows)
        floats = tokens[span, :].astype(jnp.float32)
        mean = jnp.mean(floats * floats, axis=-1, keepdims=True)
        normed[span, :] = (
            floats * lax.rsqrt(mean + norm_eps) * gain[...].astype(jnp.float32)
        ).astype(normed.dtype)
        return carry

    lax.fori_loop(0, 8, normalise, 0)
    for index in early:
        arrival(index, partner)
        pair_copies(index, start)
    for step in range(1, lines):
        for index in range(count):
            step_copies(index, step, start, True)

    rows = normed.shape[0] // 2

    complete(0)
    down = down_all[...].reshape(-1, down_all.shape[2])
    shrunk = lax.dot_general(
        normed[...], down, (((1,), (1,)), ((), ())), preferred_element_type=jnp.float32
    ).astype(jnp.bfloat16)
    shrunk_out[...] = jnp.dot(
        shrunk * mask[...], fold[...], preferred_element_type=jnp.float32
    ).astype(jnp.bfloat16)
    for hop in range(1, tp_total):
        shrunk_copy(hop).start()
    complete(1)
    for index, result in ((2, query_out), (3, key_out), (4, value_out)):
        complete(index)

        def one(piece, carry):
            span = pl.ds(pl.multiple_of(piece * rows, rows), rows)
            weight = gathered[index][...].reshape(-1, gathered[index].shape[2])
            result[span, :] = jnp.dot(
                normed[span, :], weight, preferred_element_type=jnp.float32
            )
            return carry

        lax.fori_loop(0, 2, one, 0)
    for hop in range(1, tp_total):
        shrunk_copy(hop).wait()
    total = shrunk_out[...]
    for hop in range(1, tp_total):
        total = total + shrunk_got[hop - 1]
    shrunk_out[...] = total
    complete(5)
    for index in range(count):
        own_copies(index, finish)
        if index in early:
            pair_copies(index, finish)
        for step in range(1, lines):
            step_copies(index, step, finish, False)


def relay_project(arrays, tokens, gain, mask, fold, req_total, tp_total):
    lines = req_total // 2
    axes = (0, 0, 0, 0, 0, 1)
    count = len(arrays)
    up, weight, output = arrays[1], arrays[2], arrays[5]
    row_total = tokens.shape[0]
    base = jax.ShapeDtypeStruct((row_total, weight.shape[1]), jnp.float32)
    whole = pltpu.VMEM((req_total,) + weight.shape, weight.dtype)
    in_vmem = pl.BlockSpec(memory_space=pltpu.VMEM)
    anywhere = pl.BlockSpec(memory_space=pl.ANY)
    return pl.pallas_call(
        functools.partial(relay_kernel, lines, axes, (0, 1), tp_total),
        out_shape=[
            jax.ShapeDtypeStruct((req_total,) + up.shape, up.dtype),
            jax.ShapeDtypeStruct((output.shape[0], req_total * output.shape[1]), output.dtype),
            base,
            base,
            base,
            jax.ShapeDtypeStruct((row_total, fold.shape[1]), jnp.bfloat16),
        ],
        in_specs=[pl.BlockSpec(memory_space=pltpu.HBM)] * count + [in_vmem] * 4,
        out_specs=[anywhere] * 2 + [in_vmem] * 4,
        scratch_shapes=[
            pltpu.VMEM((req_total,) + arrays[0].shape, arrays[0].dtype),
            whole,
            whole,
            whole,
            pltpu.VMEM((tp_total - 1, row_total, fold.shape[1]), jnp.bfloat16),
            pltpu.VMEM(tokens.shape, jnp.bfloat16),
            pltpu.SemaphoreType.DMA((count, 5 + 4 * (lines - 1))),
            pltpu.SemaphoreType.DMA((count, req_total)),
            pltpu.SemaphoreType.DMA((count,)),
            pltpu.SemaphoreType.DMA((tp_total - 1,)),
            pltpu.SemaphoreType.DMA((tp_total - 1,)),
        ],
        compiler_params=pltpu.CompilerParams(
            collective_id=0, has_side_effects=True, vmem_limit_bytes=58 * 1024 * 1024
        ),
    )(*arrays, tokens, gain, mask, fold)


def project_kernel(
    attended, weight, residual, out, sent_far, sent_near, sent_across, got_far, got_near, got_across,
    send_sems, recv_sems,
):
    me = lax.axis_index("tp")
    near = me + 1 - 2 * lax.rem(me, 2)
    across = lax.rem(me + 2, 4)
    far = lax.rem(near + 2, 4)
    width = out.shape[1]
    chunks = sent_far.shape[0]
    rows = sent_far.shape[1]

    def product(chunk, target):
        columns = pl.ds(pl.multiple_of(target * width, width), width)
        return jnp.dot(
            attended[pl.ds(chunk * rows, rows), :],
            weight[:, columns],
            preferred_element_type=jnp.float32,
        )

    def copy(kind, sent, got, chunk, target):
        return pltpu.make_async_remote_copy(
            src_ref=sent.at[chunk],
            dst_ref=got.at[chunk],
            send_sem=send_sems.at[kind, chunk],
            recv_sem=recv_sems.at[kind, chunk],
            device_id={"tp": target},
            device_id_type=pl.DeviceIdType.MESH,
        )

    def far_copy(chunk):
        return copy(0, sent_far, got_far, chunk, near)

    def near_copy(chunk):
        return copy(1, sent_near, got_near, chunk, near)

    def across_copy(chunk):
        return copy(2, sent_across, got_across, chunk, across)

    barrier = pltpu.get_barrier_semaphore()
    for target in (near, across):
        pl.semaphore_signal(
            barrier, inc=1, device_id={"tp": target}, device_id_type=pl.DeviceIdType.MESH
        )
    pl.semaphore_wait(barrier, 2)
    for chunk in range(chunks):
        sent_far[chunk] = product(chunk, far).astype(sent_far.dtype)
        far_copy(chunk).start()
    for chunk in range(chunks):
        mine = product(chunk, across)
        far_copy(chunk).wait_recv()
        sent_across[chunk] = (mine + got_far[chunk].astype(jnp.float32)).astype(sent_across.dtype)
        across_copy(chunk).start()
    for chunk in range(chunks):
        sent_near[chunk] = product(chunk, near).astype(sent_near.dtype)
        near_copy(chunk).start()
    for chunk in range(chunks):
        span = pl.ds(chunk * rows, rows)
        total = product(chunk, me) + residual[span, :].astype(jnp.float32)
        near_copy(chunk).wait_recv()
        total = total + got_near[chunk].astype(jnp.float32)
        across_copy(chunk).wait_recv()
        out[span, :] = (total + got_across[chunk].astype(jnp.float32)).astype(out.dtype)
    for chunk in range(chunks):
        far_copy(chunk).wait_send()
        across_copy(chunk).wait_send()
        near_copy(chunk).wait_send()


def project_and_scatter(attended, weight, residual):
    row_total = attended.shape[0]
    width = residual.shape[1]
    chunks = 4
    piece = pltpu.VMEM((chunks, row_total // chunks, width), jnp.bfloat16)
    return pl.pallas_call(
        project_kernel,
        out_shape=jax.ShapeDtypeStruct(residual.shape, residual.dtype),
        in_specs=[pl.BlockSpec(memory_space=pltpu.VMEM)] * 3,
        out_specs=pl.BlockSpec(memory_space=pltpu.VMEM),
        scratch_shapes=[piece] * 6
        + [pltpu.SemaphoreType.DMA((3, chunks)), pltpu.SemaphoreType.DMA((3, chunks))],
        compiler_params=pltpu.CompilerParams(
            collective_id=1, has_side_effects=True, vmem_limit_bytes=32 * 1024 * 1024
        ),
    )(attended, weight, residual)


def active_rows(stored, active_slots):
    slot_total = stored.shape[0]
    own = (active_slots // slot_total) == lax.axis_index("req")
    rows = jnp.where(
        own[:, None, None],
        jnp.take(stored, active_slots % slot_total, axis=0),
        jnp.zeros((), stored.dtype),
    )
    return lax.psum(rows, "req").reshape(-1, stored.shape[2])


def positions_of(segment):
    ordinal = jnp.arange(segment.shape[0], dtype=jnp.int32)
    starts = jnp.concatenate([jnp.ones((1,), jnp.bool_), segment[1:] != segment[:-1]])
    segment_start = lax.cummax(jnp.where(starts, ordinal, jnp.zeros_like(ordinal)), axis=0)
    return ordinal - segment_start


def apply_rotation(values, token_positions):
    half_dim = HEAD_WIDTH // 2
    frequency = rope_base ** (-(jnp.arange(half_dim, dtype=jnp.float32) * 2.0 / HEAD_WIDTH))
    angles = token_positions.astype(jnp.float32)[:, None] * frequency[None, :]
    cosine = jnp.cos(angles)[:, None, :]
    sine_part = jnp.sin(angles)[:, None, :]
    first_half = values[..., :half_dim]
    second_half = values[..., half_dim:]
    return jnp.concatenate(
        [
            first_half * cosine - second_half * sine_part,
            second_half * cosine + first_half * sine_part,
        ],
        axis=-1,
    )


def attend(query_per_head, key_heads, value_per_head, segment):
    scores = (
        jnp.einsum("qhd,khd->hqk", query_per_head, key_heads, preferred_element_type=jnp.float32)
        * 0.125
    )
    ordinal = jnp.arange(segment.shape[0], dtype=jnp.int32)
    allowed = (segment[:, None] == segment[None, :]) & (ordinal[None, :] <= ordinal[:, None])
    scores = jnp.where(allowed[None], scores, jnp.float32(-1e30))
    row_peak = jnp.max(scores, axis=-1, keepdims=True)
    exponent = jnp.where(allowed[None], jnp.exp(scores - row_peak), jnp.float32(0.0))
    weights = (exponent / jnp.sum(exponent, axis=-1, keepdims=True)).astype(jnp.bfloat16)
    return jnp.einsum(
        "hqk,khd->qhd", weights, value_per_head, preferred_element_type=jnp.float32
    ).astype(jnp.bfloat16)


def local(
    tokens,
    token_request_number,
    request_adapter_position,
    adapters_in_use,
    adapter_storage_slot,
    input_norm_gain,
    query_weight,
    key_weight,
    value_weight,
    output_weight,
    adapter_down_weight,
    adapter_up_weight,
):
    row_total, model_width = tokens.shape
    local_width = query_weight.shape[1]
    reduced_rows = adapter_down_weight.shape[2]
    slot_total = adapter_down_weight.shape[0]
    segment = token_request_number[0]
    request_adapters = request_adapter_position[0]
    tp_total = lax.axis_size("tp")
    req_total = lax.axis_size("req")
    part_rows = reduced_rows // tp_total
    share = 2 * part_rows
    down_part = lax.dynamic_slice_in_dim(
        adapter_down_weight, lax.axis_index("tp") * part_rows, part_rows, 2
    ).reshape(slot_total, share, model_width)
    up_part = adapter_up_weight.reshape(slot_total, 2 * reduced_rows, local_width)
    active_slots = jnp.take(adapter_storage_slot, adapters_in_use, axis=0)
    relayed = req_total % 2 == 0 and req_total <= 16
    relayed = relayed and slot_total * req_total <= 2 * active_slots.shape[0]
    if relayed:
        place_total = slot_total * req_total
        request_places = active_slots[request_adapters]
    else:
        place_total = active_slots.shape[0]
        request_places = request_adapters
    member = segment[:, None] == jnp.arange(request_adapters.shape[0], dtype=jnp.int32)[None, :]
    token_place = jnp.sum(
        jnp.where(member, request_places[None, :], jnp.zeros_like(request_places)[None, :]),
        axis=1,
    )
    column = jnp.arange(place_total * share, dtype=jnp.int32)
    mask = (token_place[:, None] == (column // share)[None, :]).astype(jnp.bfloat16)
    lanes = max(128, tp_total * share)
    fold = (lax.axis_index("tp") * share + column % share)[:, None] == jnp.arange(
        lanes, dtype=jnp.int32
    )[None, :]
    fold = fold.astype(jnp.bfloat16)
    if relayed:
        arrays = [
            down_part.reshape(slot_total * share, model_width),
            up_part.reshape(slot_total * 2 * reduced_rows, local_width),
            query_weight,
            key_weight,
            value_weight,
            output_weight,
        ]
        up_all, output_full, query_plain, key_base, value_plain, shrunk = relay_project(
            arrays, tokens, input_norm_gain[None, :], mask, fold, req_total, tp_total
        )
    else:
        floats = tokens.astype(jnp.float32)
        normed = (
            floats
            * lax.rsqrt(jnp.mean(floats * floats, axis=-1, keepdims=True) + norm_eps)
            * input_norm_gain.astype(jnp.float32)
        ).astype(jnp.bfloat16)
        down_all = active_rows(down_part, active_slots)
        up_all = active_rows(up_part, active_slots)
        output_full = lax.all_gather(output_weight, "req", axis=1, tiled=True)
        query_plain, key_base, value_plain = [
            jnp.dot(
                normed,
                lax.all_gather(weight, "req", axis=0, tiled=True),
                preferred_element_type=jnp.float32,
            )
            for weight in (query_weight, key_weight, value_weight)
        ]
        shrunk_all = lax.dot_general(
            normed, down_all, (((1,), (1,)), ((), ())), preferred_element_type=jnp.float32
        ).astype(jnp.bfloat16)
        shrunk = lax.psum(
            jnp.dot(shrunk_all * mask, fold, preferred_element_type=jnp.float32), "tp"
        ).astype(jnp.bfloat16)
    shrunk = shrunk[:, : tp_total * share]
    source = jnp.arange(tp_total * share, dtype=jnp.int32)
    source_kind = (source % share) // part_rows
    source_rank = (source // share) * part_rows + source % part_rows
    target = jnp.arange(place_total * reduced_rows, dtype=jnp.int32)
    mine = token_place[:, None] == (target // reduced_rows)[None, :]
    up_all = up_all.reshape(place_total, 2, reduced_rows, local_width)

    def change_of(kind):
        spread_map = (source_kind == kind)[:, None] & (
            source_rank[:, None] == (target % reduced_rows)[None, :]
        )
        spread = jnp.dot(
            shrunk, spread_map.astype(jnp.bfloat16), preferred_element_type=jnp.float32
        ).astype(jnp.bfloat16)
        spread = jnp.where(mine, spread, jnp.zeros((), jnp.bfloat16))
        return jnp.dot(
            spread,
            up_all[:, kind].reshape(place_total * reduced_rows, local_width),
            preferred_element_type=jnp.float32,
        )

    query_change = change_of(0)
    value_change = change_of(1)
    head_total = local_width // HEAD_WIDTH
    token_positions = positions_of(segment)
    query_per_head = apply_rotation(
        (query_plain + adapter_scale * query_change).reshape(row_total, head_total, HEAD_WIDTH),
        token_positions,
    ).astype(jnp.bfloat16)
    key_heads = apply_rotation(
        key_base.reshape(row_total, head_total, HEAD_WIDTH), token_positions
    ).astype(jnp.bfloat16)
    value_per_head = (
        (value_plain + adapter_scale * value_change)
        .astype(jnp.bfloat16)
        .reshape(row_total, head_total, HEAD_WIDTH)
    )
    attended = attend(query_per_head, key_heads, value_per_head, segment).reshape(
        row_total, local_width
    )
    share_width = model_width // tp_total
    residual_part = lax.dynamic_slice_in_dim(
        tokens, lax.axis_index("tp") * share_width, share_width, 1
    )
    if tp_total == 4:
        return project_and_scatter(attended, output_full, residual_part)
    partial_out = jnp.dot(attended, output_full, preferred_element_type=jnp.float32)
    summed = lax.psum_scatter(
        partial_out.astype(jnp.bfloat16), "tp", scatter_dimension=1, tiled=True
    ).astype(jnp.float32)
    return (summed + residual_part.astype(jnp.float32)).astype(jnp.bfloat16)


def solution(mesh):
    in_specs = (
        P("req", None),
        P("req", None),
        P("req", None),
        P(),
        P(),
        P(),
        P("req", "tp"),
        P("req", "tp"),
        P("req", "tp"),
        P("tp", "req"),
        P("req", None, None, None),
        P("req", None, None, "tp"),
    )
    out_specs = P("req", "tp")
    return jax.shard_map(local, mesh=mesh, in_specs=in_specs, out_specs=out_specs, check_vma=False)
```
